512 devices in a mesh: section: 8 (over y), sec: 64 (over x, z, core).
Axes of the slice: x: 4, y: 8, z: 8, core: 2. Of those that a mesh axis runs over, the one named last changes fastest.
Arguments:
- saved_inputs: bfloat16 [8, 2, 64, 128, 256], P('section', None, 'sec'), may hold values from -6 to 6
- weights: bfloat16 [8, 2304, 256], P('section', 'sec'), may hold values from -0.25 to 0.25
- biases: float32 [8, 256], P('section'), may hold values from -3 to 3
- cotangent: bfloat16 [2, 64, 128, 256], P(None, 'sec'), may hold values from -6 to 6
- tile_list: int32 [64, 6], P('sec'), may hold values from 0 to 7, as said below
- tile_count: int32 [64], P('sec'), may hold values from 1 to 6, as said below
- order: int32 [2], replicated, may hold values from 0 to 1, each once
Outputs:
- grad_inputs: bfloat16 [8, 2, 64, 128, 256], P('section', None, 'sec')
- weight_grads: float32 [8, 2304, 256], P('section', 'sec')
- bias_grads: float32 [8, 256], P('section', 'sec')
The draws below stay inside these ranges and needn't reach their ends.
Inputs may be any that keep to these rules, and one draw needn't show every extreme that they name: Each row of tile_list holds distinct tile indices; entries past the band's tile_count are other tiles and stand for nothing. `tile_count`: some row band has exactly 6 on-limb tiles. `order`: A permutation of the images.
All inputs are finite; a program needn't handle non-finite values.
Results may differ from the reference program's by a relative error of at most 0.03.
Values may be sent and summed in bfloat16 or wider, within the bound.
No kernel may reach another device: no remote copies, remote signals or barrier semaphores. Data moves between devices by JAX's collectives and lax.ppermute only.
A program may use at most 64 MiB of HBM per device.

```python
import jax
import jax.numpy as jnp
from jax import lax

C = 256
ROWS_DEV = 1
IMG_W = 128
TILE = 16
MOST = 6
MB = 2
SECTIONS = 8
BANDS = 64
HEIGHT = 64
TILES = 8


def tile_tables(key):
    base = jax.random.fold_in(key, 4242)
    first, second, third = jax.random.split(base, 3)
    spread = jax.random.randint(first, (BANDS,), 0, MOST)
    counts = 1 + spread * spread // MOST
    peak = jax.random.randint(second, (), 0, BANDS)
    counts = jnp.where(jnp.arange(BANDS) == peak, MOST, counts)
    scores = jax.random.randint(third, (BANDS, TILES), 0, 1 << 20) * TILES + jnp.arange(TILES)[None, :]
    ranked = jnp.argsort(scores, axis=1, stable=True)
    return (ranked[:, :MOST].astype(jnp.int32), counts.astype(jnp.int32))


def draw_tile_list(key, part):
    return tile_tables(key)[0]


def draw_tile_count(key, part):
    return tile_tables(key)[1]


def levels(rng, dims, cuts, smallest, top_value):
    level = 1.0
    for dim, blocks in cuts:
        draws = jax.random.uniform(jax.random.fold_in(jax.random.fold_in(rng, 6), dim), (blocks,), jnp.float32, smallest / len(cuts), top_value / len(cuts))
        level = level * jnp.repeat(jnp.exp(draws), dims[dim] // blocks).reshape((-1,) + (1,) * (len(dims) - 1 - dim))
    return level


def centred(own_key, extent, width, bound, cuts=(), kind=jnp.bfloat16):
    array = width * jax.random.normal(own_key, extent, jnp.float32)
    if cuts:
        array = array * levels(own_key, extent, cuts, -0.22, 0.18)
    return jnp.clip(array, -bound, bound).astype(kind)


def setup_inputs(seed: int = 0) -> dict:
    splits = jax.random.split(jax.random.key(seed), 8)
    saved_inputs = centred(splits[0], (SECTIONS, MB, HEIGHT, IMG_W, C), 1.0, 6.0, ((0, 8), (2, 64)))
    weights = centred(splits[1], (SECTIONS, 9 * C, C), (9 * C // 4) ** -0.5, 0.25, ((0, 8), (1, 64)))
    biases = centred(splits[2], (SECTIONS, C), 0.5, 3.0, ((0, 8),), jnp.float32)
    cotangent = centred(splits[3], (MB, HEIGHT, IMG_W, C), 1.0, 6.0, ((1, 64),))
    tile_list = draw_tile_list(jax.random.fold_in(splits[7], 71), 0)
    tile_count = draw_tile_count(jax.random.fold_in(splits[7], 71), 0)
    order = jax.random.permutation(splits[6], MB).astype(jnp.int32)
    return {"saved_inputs": saved_inputs, "weights": weights, "biases": biases, "cotangent": cotangent, "tile_list": tile_list, "tile_count": tile_count, "order": order}


def patches(padded, rows, cols):
    return jnp.concatenate([padded[..., a:a + rows, b:b + cols, :] for a in range(3) for b in range(3)], -1)


def tile_mask(tile_list, tile_count):
    slots = jnp.arange(MOST)[None, :] < tile_count[:, None]
    hit = (tile_list[:, :, None] == jnp.arange(TILES)[None, None, :]) & slots[:, :, None]
    on_tiles = jnp.any(hit, axis=1).astype(jnp.float32)
    return jnp.repeat(jnp.repeat(on_tiles, ROWS_DEV, 0), TILE, 1)


def reference(saved_inputs, weights, biases, cotangent, tile_list, tile_count, order):
    mask = tile_mask(tile_list, tile_count)[:, :, None]
    flipped = weights.reshape(SECTIONS, 9, C, C)[:, ::-1].astype(jnp.float32)
    weight_acc = [jnp.zeros((9 * C, C), jnp.float32) for section in range(SECTIONS)]
    bias_acc = [jnp.zeros((C,), jnp.float32) for section in range(SECTIONS)]
    grad_inputs = jnp.zeros((SECTIONS, MB, HEIGHT, IMG_W, C), jnp.bfloat16)
    for slot in range(MB):
        image = order[slot].astype(jnp.int32)
        upstream = cotangent[slot]
        for section in reversed(range(SECTIONS)):
            inputs = saved_inputs[section, image]
            padded = jnp.pad(inputs, ((1, 1), (1, 1), (0, 0)))
            columns = patches(padded, HEIGHT, IMG_W).reshape(-1, 9 * C)
            pre = jnp.dot(columns, weights[section], preferred_element_type=jnp.float32) + biases[section]
            sig = jax.nn.sigmoid(pre)
            gpre = upstream.reshape(-1, C).astype(jnp.float32) * mask.reshape(-1, 1) * (sig * (1.0 + pre * (1.0 - sig)))
            gpre = gpre.astype(jnp.bfloat16)
            grid = gpre.reshape(HEIGHT, IMG_W, C)
            gpad = jnp.pad(grid, ((1, 1), (1, 1), (0, 0)))
            gcols = patches(gpad, HEIGHT, IMG_W).reshape(-1, 9, C).astype(jnp.float32)
            back = jnp.einsum('nkc,kdc->nd', gcols, flipped[section])
            back = (back.reshape(HEIGHT, IMG_W, C) * mask).astype(jnp.bfloat16)
            grad_inputs = grad_inputs.at[section, image].set(back)
            weight_acc[section] = weight_acc[section] + lax.dot_general(columns, gpre, (((0,), (0,)), ((), ())), preferred_element_type=jnp.float32)
            bias_acc[section] = bias_acc[section] + jnp.sum(gpre.astype(jnp.float32), axis=0)
            upstream = back
    return grad_inputs, jnp.stack(weight_acc, 0), jnp.stack(bias_acc, 0)
```

```python
import jax
import jax.numpy as jnp
from jax import lax
from jax.experimental import pallas as pl
from jax.experimental.pallas import tpu as pltpu
from jax.sharding import Mesh
from jax.sharding import PartitionSpec as P

TILE = 16
COLS = 128
CH = 256
PART = 36
WIN = 40
GROUPS = 32
BF = jnp.bfloat16
F32 = jnp.float32
VMEM = pl.BlockSpec(memory_space=pltpu.VMEM)
SMEM = pl.BlockSpec(memory_space=pltpu.SMEM)
ALL = ("y", "x", "z", "c")
SEC = ("x", "z", "c")


def call(kernel, ins, outs, operands, aliases=None, scratch=(), flops=1, moved=1):
    return pl.pallas_call(
        kernel,
        out_shape=outs,
        in_specs=ins,
        out_specs=[VMEM] * len(outs),
        scratch_shapes=scratch,
        input_output_aliases=aliases or {},
        compiler_params=pltpu.CompilerParams(vmem_limit_bytes=24 << 20),
        cost_estimate=pl.CostEstimate(flops=flops, bytes_accessed=moved, transcendentals=0),
    )(*operands)


def out(shape, dtype):
    return jax.ShapeDtypeStruct(shape, dtype)


def from_left(x):
    return jnp.concatenate([jnp.zeros_like(x[:1]), x[:-1]], axis=0)


def from_right(x):
    return jnp.concatenate([x[1:], jnp.zeros_like(x[:1])], axis=0)


def pack_kernel(tiles, count, order, x, cot, w, pack, mask, wide, gacc, grads):
    gacc[...] = jnp.zeros_like(gacc)
    grads[...] = jnp.zeros_like(grads)
    most = tiles.shape[1]
    for tile in range(COLS // TILE):
        live = jnp.int32(0)
        for k in range(most):
            live = live | ((tiles[0, k] == tile) & (k < count[0])).astype(jnp.int32)
        value = live.astype(F32)
        mask[tile * TILE : (tile + 1) * TILE, :] = jnp.full((TILE, CH), value, F32)
    on = mask[...]
    for slot in range(2):
        pack[slot] = x[order[slot]]
        pack[2 + slot] = (cot[slot].astype(F32) * on).astype(BF)
    core = lax.axis_index("c")
    rows = w[...].astype(F32)
    gap = jnp.zeros((WIN - PART, CH), F32)
    first = jnp.concatenate([rows, gap], axis=0)
    second = jnp.concatenate([gap, rows], axis=0)
    part = jnp.where(core == 0, first, second).astype(BF)
    for k in range(GROUPS):
        wide[k] = part


def prep_kernel(mine, other, bias, own, up1, down1, up2, down2, deriv, weights):
    core = lax.axis_index("c")

    def assemble(even, odd):
        for k in range(GROUPS):
            base = 72 * k
            weights[base : base + 32] = even[k, 0:32]
            both = even[k, 32:40].astype(F32) + odd[k, 0:8].astype(F32)
            weights[base + 32 : base + 40] = both.astype(BF)
            weights[base + 40 : base + 72] = odd[k, 8:40]

    @pl.when(core == 0)
    def _():
        assemble(mine, other)

    @pl.when(core == 1)
    def _():
        assemble(other, mine)

    shift = jnp.broadcast_to(bias[...], (COLS, CH))
    for slot in range(2):
        x = jnp.concatenate([up2[slot], up1[slot], own[slot], down1[slot], down2[slot]], axis=0)
        sums = []
        for b in range(3):
            total = None
            for a in range(3):
                tap = (3 * a + b) * CH
                term = jnp.dot(
                    x[a * COLS : (a + 3) * COLS],
                    weights[tap : tap + CH],
                    preferred_element_type=F32,
                )
                total = term if total is None else total + term
            sums.append(total)
        for r in range(3):
            rows = slice(r * COLS, (r + 1) * COLS)
            pre = from_left(sums[0][rows]) + sums[1][rows] + from_right(sums[2][rows]) + shift
            sig = jax.nn.sigmoid(pre)
            deriv[slot, r] = sig * (1.0 + pre * (1.0 - sig))


def step_kernel(step, sections, *refs):
    order, mask, deriv, weights = refs[:4]
    rest = refs[4:]
    if step <= 1:
        cots, rest = rest[:3], rest[3:]
    if step >= 1:
        got, rest = rest[:3], rest[3:]
    gacc_in, grads_in, back, gacc, grads = rest
    gacc[...] = gacc_in[...]
    grads[...] = grads_in[...]
    section = lax.axis_index("y")
    slot = step - (sections - 1 - section)

    @pl.when((slot >= 0) & (slot < 2))
    def _():
        gpre = []
        for r in range(3):
            if step == 0:
                upstream = cots[r][2]
            elif step == 1:
                upstream = jnp.where(section == sections - 1, cots[r][3], got[r][...])
            else:
                upstream = got[r][...]
            gpre.append((upstream.astype(F32) * deriv[slot, r]).astype(BF))
        gacc[slot] = gpre[1]
        sums = []
        for b in range(3):
            total = None
            for a in range(3):
                tap = (3 * a + b) * CH
                term = lax.dot_general(
                    gpre[2 - a],
                    weights[tap : tap + CH],
                    (((1,), (1,)), ((), ())),
                    preferred_element_type=F32,
                )
                total = term if total is None else total + term
            sums.append(total)
        value = from_right(sums[0]) + sums[1] + from_left(sums[2])
        value = (value * mask[...]).astype(BF)
        back[...] = value
        grads[order[slot]] = value


def wgrad_kernel(own, up, down, gacc, mine, theirs, total):
    core = lax.axis_index("c")
    g = [gacc[slot].astype(F32) for slot in range(2)]
    shifted = [
        jnp.concatenate([from_right(g[0]), from_right(g[1])], axis=0).astype(BF),
        jnp.concatenate([gacc[0], gacc[1]], axis=0),
        jnp.concatenate([from_left(g[0]), from_left(g[1])], axis=0).astype(BF),
    ]
    for a, rows in enumerate((up, own, down)):
        x = jnp.concatenate([rows[0], rows[1]], axis=0)
        for b in range(3):
            tap = (3 * a + b) * CH
            total[tap : tap + CH] = lax.dot_general(
                x, shifted[b], (((0,), (0,)), ((), ())), preferred_element_type=F32
            )
    bias = jnp.sum(g[0] + g[1], axis=0, keepdims=True)
    high = bias.astype(BF).astype(F32)
    low = (bias - high).astype(BF).astype(F32)
    row = lax.broadcasted_iota(jnp.int32, (WIN, CH), 0)

    def window(which, start):
        at = jnp.where(which == 0, PART, 0)
        return total[pl.ds(pl.multiple_of(start, 8), WIN), :], at

    for k in range(GROUPS):
        value, at = window(core, 72 * k + 32 * core)
        value = jnp.where(row == at, bias, value)
        mine[k] = jnp.where(row == at + 1, 0.0, value)
        value, at = window(1 - core, 72 * k + 32 * (1 - core))
        value = jnp.where(row == at, high, value)
        theirs[k] = jnp.where(row == at + 1, low, value).astype(BF)


def pair_kernel(mine, got, both):
    core = lax.axis_index("c")
    row = lax.broadcasted_iota(jnp.int32, (WIN, CH), 0)
    at = jnp.where(core == 0, PART, 0)
    lead = mine[0] + got[0].astype(F32)
    here = (row == at) | (row == at + 1)
    bias = jnp.sum(jnp.where(here, lead, 0.0), axis=0, keepdims=True)
    high = bias.astype(BF).astype(F32)
    low = bias - high
    for k in range(GROUPS):
        value = mine[k] + got[k].astype(F32)
        value = jnp.where(row == at, high, value)
        both[k] = jnp.where(row == at + 1, low, value).astype(BF)


def total_kernel(parts, wgrad, bgrad):
    core = lax.axis_index("c")
    me = (lax.axis_index("x") * lax.axis_size("z") + lax.axis_index("z")) * 2 + core
    value = parts[0].astype(F32)
    for k in range(1, GROUPS):
        value = value + parts[k].astype(F32)
    wgrad[...] = jnp.where(core == 0, value[:PART], value[WIN - PART :])
    row = lax.broadcasted_iota(jnp.int32, (WIN, CH), 0)
    at = jnp.where(core == 0, PART, 0)
    here = (row == at) | (row == at + 1)
    bias = jnp.sum(jnp.where(here, value, 0.0), axis=0, keepdims=True)
    lane = lax.broadcasted_iota(jnp.int32, (1, CH), 1)
    spot = lax.broadcasted_iota(jnp.int32, (1, 4), 1)
    result = jnp.zeros((1, 4), F32)
    for j in range(4):
        one = jnp.sum(jnp.where(lane == 4 * me + j, bias, 0.0), axis=1, keepdims=True)
        result = jnp.where(spot == j, one, result)
    bgrad[...] = result


def shift_pairs(size, by):
    return [(s, s + by) for s in range(size) if 0 <= s + by < size]


def hop_pairs(planes, size, by):
    return [
        (p * size + s, (p - 1) * size + s + by)
        for p in planes
        for s in range(size)
        if 0 <= s + by < size
    ]


def body(saved_inputs, weights, biases, cotangent, tile_list, tile_count, order):
    sections = lax.axis_size("y")
    size = 64
    image = (2, COLS, CH)
    inputs = saved_inputs.reshape(image)
    cot = cotangent.reshape(image)

    pack, mask, wide, gacc, grads = call(
        pack_kernel,
        [SMEM, SMEM, SMEM, VMEM, VMEM, VMEM],
        [out((4, COLS, CH), BF), out((COLS, CH), F32), out((GROUPS, WIN, CH), BF)]
        + [out(image, BF)] * 2,
        (tile_list, tile_count, order, inputs, cot, weights[0]),
        moved=3 << 20,
    )
    up1 = lax.ppermute(pack, SEC, shift_pairs(size, 1))
    down1 = lax.ppermute(pack, SEC, shift_pairs(size, -1))
    xs = pack[:2]
    up2 = lax.ppermute(xs, SEC, shift_pairs(size, 2))
    down2 = lax.ppermute(xs, SEC, shift_pairs(size, -2))

    swap = [(0, 1), (1, 0)]
    mine = lax.all_to_all(wide, ("x", "z"), 0, 0)
    other = lax.ppermute(mine, "c", swap)

    deriv, wfull = call(
        prep_kernel,
        [VMEM] * 8,
        [out((2, 3, COLS, CH), F32), out((9 * CH, CH), BF)],
        (mine, other, biases, pack, up1, down1, up2, down2),
        flops=1 << 30,
        moved=4 << 20,
    )

    got = None
    for step in range(sections + 1):
        operands = [order, mask, deriv, wfull]
        if step <= 1:
            operands += [up1, pack, down1]
        if step >= 1:
            operands += got
        count = len(operands)
        back, gacc, grads = call(
            lambda *refs, step=step: step_kernel(step, sections, *refs),
            [SMEM] + [VMEM] * (count + 1),
            [out((COLS, CH), BF), out(image, BF), out(image, BF)],
            (*operands, gacc, grads),
            aliases={count: 1, count + 1: 2},
            flops=1 << 27,
            moved=2 << 20,
        )
        if step < sections:
            planes = [p for p in (sections - 1 - step, sections - step) if 0 < p < sections]
            got = [
                lax.ppermute(back, ALL, hop_pairs(planes, size, by)) for by in (1, 0, -1)
            ]

    mine, theirs = call(
        wgrad_kernel,
        [VMEM] * 4,
        [out((GROUPS, WIN, CH), F32), out((GROUPS, WIN, CH), BF)],
        (pack, up1, down1, gacc),
        scratch=[pltpu.VMEM((9 * CH, CH), F32)],
        flops=1 << 28,
        moved=4 << 20,
    )
    received = lax.ppermute(theirs, "c", swap)
    (both,) = call(
        pair_kernel,
        [VMEM] * 2,
        [out((GROUPS, WIN, CH), BF)],
        (mine, received),
        moved=3 << 20,
    )
    parts = lax.all_to_all(both, ("x", "z"), 0, 0)
    wgrad, bgrad = call(
        total_kernel,
        [VMEM],
        [out((PART, CH), F32), out((1, 4), F32)],
        (parts,),
        moved=1 << 20,
    )
    return grads.reshape(1, 2, 1, COLS, CH), wgrad[None], bgrad


def solution(mesh):
    fine = Mesh(mesh.devices.reshape(8, 4, 8, 2), ALL)
    placed = (
        P("y", None, SEC, None, None),
        P("y", SEC, None),
        P("y", None),
        P(None, SEC, None, None),
        P(SEC, None),
        P(SEC),
        P(),
    )
    return jax.shard_map(
        body,
        mesh=fine,
        in_specs=placed,
        out_specs=(P("y", None, SEC, None, None), P("y", SEC, None), P("y", SEC)),
        check_vma=False,
    )
```

```python
import jax
import jax.numpy as jnp
from jax import lax
from jax.experimental import pallas as pl
from jax.experimental.pallas import tpu as pltpu
from jax.sharding import Mesh
from jax.sharding import PartitionSpec as P

TILE = 16
COLS = 128
CH = 256
PART = 36
WIN = 40
GROUPS = 32
BF = jnp.bfloat16
F32 = jnp.float32
VMEM = pl.BlockSpec(memory_space=pltpu.VMEM)
SMEM = pl.BlockSpec(memory_space=pltpu.SMEM)
HBM = pl.BlockSpec(memory_space=pltpu.HBM)
ANY = pl.BlockSpec(memory_space=pl.ANY)
ALL = ("y", "x", "z", "c")
SEC = ("x", "z", "c")


def call(kernel, ins, outs, operands, aliases=None, scratch=(), flops=1, moved=1):
    return pl.pallas_call(
        kernel,
        out_shape=outs,
        in_specs=ins,
        out_specs=[VMEM] * len(outs),
        scratch_shapes=scratch,
        input_output_aliases=aliases or {},
        compiler_params=pltpu.CompilerParams(vmem_limit_bytes=24 << 20),
        cost_estimate=pl.CostEstimate(flops=flops, bytes_accessed=moved, transcendentals=0),
    )(*operands)


def out(shape, dtype):
    return jax.ShapeDtypeStruct(shape, dtype)


def from_left(x):
    return jnp.concatenate([jnp.zeros_like(x[:1]), x[:-1]], axis=0)


def from_right(x):
    return jnp.concatenate([x[1:], jnp.zeros_like(x[:1])], axis=0)


def pack_kernel(order, count, tiles, x, cot, w, pack, xs, mask, part, state, cotv, wv, tv, sems):
    copies = [
        pltpu.make_async_copy(tiles, tv, sems.at[0]),
        pltpu.make_async_copy(cot, cotv, sems.at[1]),
        pltpu.make_async_copy(w, wv, sems.at[2]),
    ]
    for slot in range(2):
        source = x.at[order[slot]]
        copies.append(pltpu.make_async_copy(source, xs.at[slot], sems.at[3 + slot]))
        copies.append(pltpu.make_async_copy(source, pack.at[slot], sems.at[5 + slot]))
    for copy in copies:
        copy.start()
    state[...] = jnp.zeros_like(state)
    copies[0].wait()
    most = tiles.shape[1]
    for tile in range(COLS // TILE):
        live = jnp.int32(0)
        for k in range(most):
            live = live | ((tv[0, k] == tile) & (k < count[0])).astype(jnp.int32)
        value = live.astype(F32)
        mask[tile * TILE : (tile + 1) * TILE, :] = jnp.full((TILE, CH), value, F32)
    copies[1].wait()
    on = mask[...]
    for slot in range(2):
        pack[2 + slot] = (cotv[slot].astype(F32) * on).astype(BF)
    copies[2].wait()
    core = lax.axis_index("c")
    rows = wv[...].astype(F32)
    gap = jnp.zeros((WIN - PART, CH), F32)
    first = jnp.concatenate([rows, gap], axis=0)
    second = jnp.concatenate([gap, rows], axis=0)
    part[...] = jnp.where(core == 0, first, second).astype(BF)
    for copy in copies[3:]:
        copy.wait()


def wide_kernel(part, *refs):
    wide = refs[-1]
    value = part[...]
    for k in range(GROUPS):
        wide[k] = value


def prep_kernel(mine, other, bias, own, up1, down1, up2, down2, deriv, weights):
    core = lax.axis_index("c")

    def assemble(even, odd):
        for k in range(GROUPS):
            base = 72 * k
            weights[base : base + 32] = even[k, 0:32]
            both = even[k, 32:40].astype(F32) + odd[k, 0:8].astype(F32)
            weights[base + 32 : base + 40] = both.astype(BF)
            weights[base + 40 : base + 72] = odd[k, 8:40]

    @pl.when(core == 0)
    def _():
        assemble(mine, other)

    @pl.when(core == 1)
    def _():
        assemble(other, mine)

    shift = jnp.broadcast_to(bias[...], (COLS, CH))
    for slot in range(2):
        x = jnp.concatenate([up2[slot], up1[slot], own[slot], down1[slot], down2[slot]], axis=0)
        sums = []
        for b in range(3):
            total = None
            for a in range(3):
                tap = (3 * a + b) * CH
                term = jnp.dot(
                    x[a * COLS : (a + 3) * COLS],
                    weights[tap : tap + CH],
                    preferred_element_type=F32,
                )
                total = term if total is None else total + term
            sums.append(total)
        for r in range(3):
            rows = slice(r * COLS, (r + 1) * COLS)
            pre = from_left(sums[0][rows]) + sums[1][rows] + from_right(sums[2][rows]) + shift
            sig = jax.nn.sigmoid(pre)
            deriv[slot, r] = sig * (1.0 + pre * (1.0 - sig))


def step_kernel(step, sections, *refs):
    mask, deriv, weights = refs[:3]
    rest = refs[3:]
    if step <= 1:
        cots, rest = rest[:3], rest[3:]
    if step >= 1:
        got, rest = rest[:3], rest[3:]
    state_in, back, state = rest
    state[...] = state_in[...]
    section = lax.axis_index("y")
    slot = step - (sections - 1 - section)

    @pl.when((slot >= 0) & (slot < 2))
    def _():
        gpre = []
        for r in range(3):
            if step == 0:
                upstream = cots[r][2]
            elif step == 1:
                upstream = jnp.where(section == sections - 1, cots[r][3], got[r][...])
            else:
                upstream = got[r][...]
            gpre.append((upstream.astype(F32) * deriv[slot, r]).astype(BF))
        state[slot] = gpre[1]
        sums = []
        for b in range(3):
            total = None
            for a in range(3):
                tap = (3 * a + b) * CH
                term = lax.dot_general(
                    gpre[2 - a],
                    weights[tap : tap + CH],
                    (((1,), (1,)), ((), ())),
                    preferred_element_type=F32,
                )
                total = term if total is None else total + term
            sums.append(total)
        value = from_right(sums[0]) + sums[1] + from_left(sums[2])
        value = (value * mask[...]).astype(BF)
        back[...] = value
        state[2 + slot] = value


def grads_kernel(order, state, grads):
    for slot in range(2):
        grads[order[slot]] = state[2 + slot]


def wgrad_kernel(own, up, down, gacc, mine, theirs, total):
    core = lax.axis_index("c")
    g = [gacc[slot].astype(F32) for slot in range(2)]
    shifted = [
        jnp.concatenate([from_right(g[0]), from_right(g[1])], axis=0).astype(BF),
        jnp.concatenate([gacc[0], gacc[1]], axis=0),
        jnp.concatenate([from_left(g[0]), from_left(g[1])], axis=0).astype(BF),
    ]
    for a, rows in enumerate((up, own, down)):
        x = jnp.concatenate([rows[0], rows[1]], axis=0)
        for b in range(3):
            tap = (3 * a + b) * CH
            total[tap : tap + CH] = lax.dot_general(
                x, shifted[b], (((0,), (0,)), ((), ())), preferred_element_type=F32
            )
    bias = jnp.sum(g[0] + g[1], axis=0, keepdims=True)
    high = bias.astype(BF).astype(F32)
    low = (bias - high).astype(BF).astype(F32)
    row = lax.broadcasted_iota(jnp.int32, (WIN, CH), 0)

    def window(which, start):
        at = jnp.where(which == 0, PART, 0)
        return total[pl.ds(pl.multiple_of(start, 8), WIN), :], at

    for k in range(GROUPS):
        value, at = window(core, 72 * k + 32 * core)
        value = jnp.where(row == at, bias, value)
        mine[k] = jnp.where(row == at + 1, 0.0, value)
        value, at = window(1 - core, 72 * k + 32 * (1 - core))
        value = jnp.where(row == at, high, value)
        theirs[k] = jnp.where(row == at + 1, low, value).astype(BF)


def pair_kernel(mine, got, both):
    core = lax.axis_index("c")
    row = lax.broadcasted_iota(jnp.int32, (WIN, CH), 0)
    at = jnp.where(core == 0, PART, 0)
    lead = mine[0] + got[0].astype(F32)
    here = (row == at) | (row == at + 1)
    bias = jnp.sum(jnp.where(here, lead, 0.0), axis=0, keepdims=True)
    high = bias.astype(BF).astype(F32)
    low = bias - high
    for k in range(GROUPS):
        value = mine[k] + got[k].astype(F32)
        value = jnp.where(row == at, high, value)
        both[k] = jnp.where(row == at + 1, low, value).astype(BF)


def total_kernel(parts, wgrad, bgrad):
    core = lax.axis_index("c")
    me = (lax.axis_index("x") * lax.axis_size("z") + lax.axis_index("z")) * 2 + core
    value = parts[0].astype(F32)
    for k in range(1, GROUPS):
        value = value + parts[k].astype(F32)
    wgrad[...] = jnp.where(core == 0, value[:PART], value[WIN - PART :])
    row = lax.broadcasted_iota(jnp.int32, (WIN, CH), 0)
    at = jnp.where(core == 0, PART, 0)
    here = (row == at) | (row == at + 1)
    bias = jnp.sum(jnp.where(here, value, 0.0), axis=0, keepdims=True)
    lane = lax.broadcasted_iota(jnp.int32, (1, CH), 1)
    spot = lax.broadcasted_iota(jnp.int32, (1, 4), 1)
    result = jnp.zeros((1, 4), F32)
    for j in range(4):
        one = jnp.sum(jnp.where(lane == 4 * me + j, bias, 0.0), axis=1, keepdims=True)
        result = jnp.where(spot == j, one, result)
    bgrad[...] = result


def shift_pairs(size, by):
    return [(s, s + by) for s in range(size) if 0 <= s + by < size]


def hop_pairs(planes, size, by):
    return [
        (p * size + s, (p - 1) * size + s + by)
        for p in planes
        for s in range(size)
        if 0 <= s + by < size
    ]


def body(saved_inputs, weights, biases, cotangent, tile_list, tile_count, order):
    sections = lax.axis_size("y")
    size = 64
    image = (2, COLS, CH)
    inputs = saved_inputs.reshape(image)
    cot = cotangent.reshape(image)

    pack, xs, mask, part, state = call(
        pack_kernel,
        [SMEM, SMEM] + [HBM] * 4,
        [
            out((4, COLS, CH), BF),
            out(image, BF),
            out((COLS, CH), F32),
            out((WIN, CH), BF),
            out((4, COLS, CH), BF),
        ],
        (order, tile_count, tile_list, inputs, cot, weights[0]),
        scratch=[
            pltpu.VMEM(image, BF),
            pltpu.VMEM((PART, CH), BF),
            pltpu.SMEM(tile_list.shape, jnp.int32),
            pltpu.SemaphoreType.DMA((7,)),
        ],
        moved=3 << 20,
    )
    up1 = lax.ppermute(pack, SEC, shift_pairs(size, 1))
    down1 = lax.ppermute(pack, SEC, shift_pairs(size, -1))
    up2 = lax.ppermute(xs, SEC, shift_pairs(size, 2))
    down2 = lax.ppermute(xs, SEC, shift_pairs(size, -2))
    (wide,) = call(
        wide_kernel,
        [VMEM] + [ANY] * 4,
        [out((GROUPS, WIN, CH), BF)],
        (part, up1, down1, up2, down2),
        moved=1 << 20,
    )

    swap = [(0, 1), (1, 0)]
    mine = lax.all_to_all(wide, ("x", "z"), 0, 0)
    other = lax.ppermute(mine, "c", swap)

    deriv, wfull = call(
        prep_kernel,
        [VMEM] * 8,
        [out((2, 3, COLS, CH), F32), out((9 * CH, CH), BF)],
        (mine, other, biases, pack, up1, down1, up2, down2),
        flops=1 << 30,
        moved=4 << 20,
    )

    got = None
    for step in range(sections + 1):
        operands = [mask, deriv, wfull]
        if step <= 1:
            operands += [up1, pack, down1]
        if step >= 1:
            operands += got
        count = len(operands)
        back, state = call(
            lambda *refs, step=step: step_kernel(step, sections, *refs),
            [VMEM] * (count + 1),
            [out((COLS, CH), BF), out((4, COLS, CH), BF)],
            (*operands, state),
            aliases={count: 1},
            flops=1 << 27,
            moved=2 << 20,
        )
        if step < sections:
            planes = [p for p in (sections - 1 - step, sections - step) if 0 < p < sections]
            got = [
                lax.ppermute(back, ALL, hop_pairs(planes, size, by)) for by in (1, 0, -1)
            ]

    mine, theirs = call(
        wgrad_kernel,
        [VMEM] * 4,
        [out((GROUPS, WIN, CH), F32), out((GROUPS, WIN, CH), BF)],
        (pack, up1, down1, state),
        scratch=[pltpu.VMEM((9 * CH, CH), F32)],
        flops=1 << 28,
        moved=4 << 20,
    )
    received = lax.ppermute(theirs, "c", swap)
    (grads,) = call(grads_kernel, [SMEM, VMEM], [out(image, BF)], (order, state), moved=1 << 18)
    (both,) = call(
        pair_kernel,
        [VMEM] * 2,
        [out((GROUPS, WIN, CH), BF)],
        (mine, received),
        moved=3 << 20,
    )
    parts = lax.all_to_all(both, ("x", "z"), 0, 0)
    wgrad, bgrad = call(
        total_kernel,
        [VMEM],
        [out((PART, CH), F32), out((1, 4), F32)],
        (parts,),
        moved=1 << 20,
    )
    return grads.reshape(1, 2, 1, COLS, CH), wgrad[None], bgrad


def solution(mesh):
    fine = Mesh(mesh.devices.reshape(8, 4, 8, 2), ALL)
    placed = (
        P("y", None, SEC, None, None),
        P("y", SEC, None),
        P("y", None),
        P(None, SEC, None, None),
        P(SEC, None),
        P(SEC),
        P(),
    )
    return jax.shard_map(
        body,
        mesh=fine,
        in_specs=placed,
        out_specs=(P("y", None, SEC, None, None), P("y", SEC, None), P("y", SEC)),
        check_vma=False,
    )
```

```python
import jax
import jax.numpy as jnp
from jax import lax
from jax.experimental import pallas as pl
from jax.experimental.pallas import tpu as pltpu
from jax.sharding import Mesh
from jax.sharding import PartitionSpec as P

TILE = 16
COLS = 128
CH = 256
PART = 36
WIN = 40
GROUPS = 32
BF = jnp.bfloat16
F32 = jnp.float32
VMEM = pl.BlockSpec(memory_space=pltpu.VMEM)
SMEM = pl.BlockSpec(memory_space=pltpu.SMEM)
HBM = pl.BlockSpec(memory_space=pltpu.HBM)
ANY = pl.BlockSpec(memory_space=pl.ANY)
ALL = ("y", "x", "z", "c")
SEC = ("x", "z", "c")


def call(kernel, ins, outs, operands, aliases=None, scratch=(), flops=1, moved=1):
    return pl.pallas_call(
        kernel,
        out_shape=outs,
        in_specs=ins,
        out_specs=[VMEM] * len(outs),
        scratch_shapes=scratch,
        input_output_aliases=aliases or {},
        compiler_params=pltpu.CompilerParams(vmem_limit_bytes=24 << 20),
        cost_estimate=pl.CostEstimate(flops=flops, bytes_accessed=moved, transcendentals=0),
    )(*operands)


def out(shape, dtype):
    return jax.ShapeDtypeStruct(shape, dtype)


def from_left(x):
    return jnp.concatenate([jnp.zeros_like(x[:1]), x[:-1]], axis=0)


def from_right(x):
    return jnp.concatenate([x[1:], jnp.zeros_like(x[:1])], axis=0)


def wide_kernel(w, wide):
    core = lax.axis_index("c")
    rows = w[...].astype(F32)
    gap = jnp.zeros((WIN - PART, CH), F32)
    first = jnp.concatenate([rows, gap], axis=0)
    second = jnp.concatenate([gap, rows], axis=0)
    part = jnp.where(core == 0, first, second).astype(BF)
    for k in range(GROUPS):
        wide[k] = part


def pack_kernel(order, count, tiles, x, cot, pack, xs, mask, state):
    state[...] = jnp.zeros_like(state)
    most = tiles.shape[1]
    for tile in range(COLS // TILE):
        live = jnp.int32(0)
        for k in range(most):
            live = live | ((tiles[0, k] == tile) & (k < count[0])).astype(jnp.int32)
        value = live.astype(F32)
        mask[tile * TILE : (tile + 1) * TILE, :] = jnp.full((TILE, CH), value, F32)
    on = mask[...]
    for slot in range(2):
        image = x[order[slot]]
        xs[slot] = image
        pack[slot] = image
        pack[2 + slot] = (cot[slot].astype(F32) * on).astype(BF)


def prep_kernel(mine, other, bias, own, up1, down1, up2, down2, deriv, weights):
    core = lax.axis_index("c")

    def assemble(even, odd):
        for k in range(GROUPS):
            base = 72 * k
            weights[base : base + 32] = even[k, 0:32]
            both = even[k, 32:40].astype(F32) + odd[k, 0:8].astype(F32)
            weights[base + 32 : base + 40] = both.astype(BF)
            weights[base + 40 : base + 72] = odd[k, 8:40]

    @pl.when(core == 0)
    def _():
        assemble(mine, other)

    @pl.when(core == 1)
    def _():
        assemble(other, mine)

    shift = jnp.broadcast_to(bias[...], (COLS, CH))
    for slot in range(2):
        x = jnp.concatenate([up2[slot], up1[slot], own[slot], down1[slot], down2[slot]], axis=0)
        sums = []
        for b in range(3):
            total = None
            for a in range(3):
                tap = (3 * a + b) * CH
                term = jnp.dot(
                    x[a * COLS : (a + 3) * COLS],
                    weights[tap : tap + CH],
                    preferred_element_type=F32,
                )
                total = term if total is None else total + term
            sums.append(total)
        for r in range(3):
            rows = slice(r * COLS, (r + 1) * COLS)
            pre = from_left(sums[0][rows]) + sums[1][rows] + from_right(sums[2][rows]) + shift
            sig = jax.nn.sigmoid(pre)
            deriv[slot, r] = sig * (1.0 + pre * (1.0 - sig))


def step_kernel(step, sections, *refs):
    mask, deriv, weights = refs[:3]
    rest = refs[3:]
    if step <= 1:
        cots, rest = rest[:3], rest[3:]
    if step >= 1:
        got, rest = rest[:3], rest[3:]
    state_in, back, state = rest
    state[...] = state_in[...]
    section = lax.axis_index("y")
    slot = step - (sections - 1 - section)

    @pl.when((slot >= 0) & (slot < 2))
    def _():
        gpre = []
        for r in range(3):
            if step == 0:
                upstream = cots[r][2]
            elif step == 1:
                upstream = jnp.where(section == sections - 1, cots[r][3], got[r][...])
            else:
                upstream = got[r][...]
            gpre.append((upstream.astype(F32) * deriv[slot, r]).astype(BF))
        state[slot] = gpre[1]
        sums = []
        for b in range(3):
            total = None
            for a in range(3):
                tap = (3 * a + b) * CH
                term = lax.dot_general(
                    gpre[2 - a],
                    weights[tap : tap + CH],
                    (((1,), (1,)), ((), ())),
                    preferred_element_type=F32,
                )
                total = term if total is None else total + term
            sums.append(total)
        value = from_right(sums[0]) + sums[1] + from_left(sums[2])
        value = (value * mask[...]).astype(BF)
        back[...] = value
        state[2 + slot] = value


def grads_kernel(order, state, grads):
    for slot in range(2):
        grads[order[slot]] = state[2 + slot]


def wgrad_kernel(own, up, down, gacc, mine, theirs, total):
    core = lax.axis_index("c")
    g = [gacc[slot].astype(F32) for slot in range(2)]
    shifted = [
        jnp.concatenate([from_right(g[0]), from_right(g[1])], axis=0).astype(BF),
        jnp.concatenate([gacc[0], gacc[1]], axis=0),
        jnp.concatenate([from_left(g[0]), from_left(g[1])], axis=0).astype(BF),
    ]
    for a, rows in enumerate((up, own, down)):
        x = jnp.concatenate([rows[0], rows[1]], axis=0)
        for b in range(3):
            tap = (3 * a + b) * CH
            total[tap : tap + CH] = lax.dot_general(
                x, shifted[b], (((0,), (0,)), ((), ())), preferred_element_type=F32
            )
    bias = jnp.sum(g[0] + g[1], axis=0, keepdims=True)
    high = bias.astype(BF).astype(F32)
    low = (bias - high).astype(BF).astype(F32)
    row = lax.broadcasted_iota(jnp.int32, (WIN, CH), 0)

    def window(which, start):
        at = jnp.where(which == 0, PART, 0)
        return total[pl.ds(pl.multiple_of(start, 8), WIN), :], at

    for k in range(GROUPS):
        value, at = window(core, 72 * k + 32 * core)
        value = jnp.where(row == at, bias, value)
        mine[k] = jnp.where(row == at + 1, 0.0, value)
        value, at = window(1 - core, 72 * k + 32 * (1 - core))
        value = jnp.where(row == at, high, value)
        theirs[k] = jnp.where(row == at + 1, low, value).astype(BF)


def pair_kernel(mine, got, both):
    core = lax.axis_index("c")
    row = lax.broadcasted_iota(jnp.int32, (WIN, CH), 0)
    at = jnp.where(core == 0, PART, 0)
    lead = mine[0] + got[0].astype(F32)
    here = (row == at) | (row == at + 1)
    bias = jnp.sum(jnp.where(here, lead, 0.0), axis=0, keepdims=True)
    high = bias.astype(BF).astype(F32)
    low = bias - high
    for k in range(GROUPS):
        value = mine[k] + got[k].astype(F32)
        value = jnp.where(row == at, high, value)
        both[k] = jnp.where(row == at + 1, low, value).astype(BF)


def total_kernel(parts, wgrad, bgrad):
    core = lax.axis_index("c")
    me = (lax.axis_index("x") * lax.axis_size("z") + lax.axis_index("z")) * 2 + core
    value = parts[0].astype(F32)
    for k in range(1, GROUPS):
        value = value + parts[k].astype(F32)
    wgrad[...] = jnp.where(core == 0, value[:PART], value[WIN - PART :])
    row = lax.broadcasted_iota(jnp.int32, (WIN, CH), 0)
    at = jnp.where(core == 0, PART, 0)
    here = (row == at) | (row == at + 1)
    bias = jnp.sum(jnp.where(here, value, 0.0), axis=0, keepdims=True)
    lane = lax.broadcasted_iota(jnp.int32, (1, CH), 1)
    spot = lax.broadcasted_iota(jnp.int32, (1, 4), 1)
    result = jnp.zeros((1, 4), F32)
    for j in range(4):
        one = jnp.sum(jnp.where(lane == 4 * me + j, bias, 0.0), axis=1, keepdims=True)
        result = jnp.where(spot == j, one, result)
    bgrad[...] = result


def shift_pairs(size, by):
    return [(s, s + by) for s in range(size) if 0 <= s + by < size]


def hop_pairs(planes, size, by):
    return [
        (p * size + s, (p - 1) * size + s + by)
        for p in planes
        for s in range(size)
        if 0 <= s + by < size
    ]


def body(saved_inputs, weights, biases, cotangent, tile_list, tile_count, order):
    sections = lax.axis_size("y")
    size = 64
    image = (2, COLS, CH)
    inputs = saved_inputs.reshape(image)
    cot = cotangent.reshape(image)

    (wide,) = call(
        wide_kernel, [VMEM], [out((GROUPS, WIN, CH), BF)], (weights[0],), moved=1 << 20
    )
    swap = [(0, 1), (1, 0)]
    mine = lax.all_to_all(wide, ("x", "z"), 0, 0)

    pack, xs, mask, state = call(
        pack_kernel,
        [SMEM] * 3 + [VMEM] * 2,
        [
            out((4, COLS, CH), BF),
            out(image, BF),
            out((COLS, CH), F32),
            out((4, COLS, CH), BF),
        ],
        (order, tile_count, tile_list, inputs, cot),
        flops=1 << 28,
        moved=3 << 20,
    )
    up1 = lax.ppermute(pack, SEC, shift_pairs(size, 1))
    down1 = lax.ppermute(pack, SEC, shift_pairs(size, -1))
    up2 = lax.ppermute(xs, SEC, shift_pairs(size, 2))
    down2 = lax.ppermute(xs, SEC, shift_pairs(size, -2))
    mine, up1, down1, up2, down2 = lax.optimization_barrier((mine, up1, down1, up2, down2))
    other = lax.ppermute(mine, "c", swap)

    deriv, wfull = call(
        prep_kernel,
        [VMEM] * 8,
        [out((2, 3, COLS, CH), F32), out((9 * CH, CH), BF)],
        (mine, other, biases, pack, up1, down1, up2, down2),
        flops=1 << 30,
        moved=4 << 20,
    )

    got = None
    for step in range(sections + 1):
        operands = [mask, deriv, wfull]
        if step <= 1:
            operands += [up1, pack, down1]
        if step >= 1:
            operands += got
        count = len(operands)
        back, state = call(
            lambda *refs, step=step: step_kernel(step, sections, *refs),
            [VMEM] * (count + 1),
            [out((COLS, CH), BF), out((4, COLS, CH), BF)],
            (*operands, state),
            aliases={count: 1},
            flops=1 << 27,
            moved=2 << 20,
        )
        if step < sections:
            planes = [p for p in (sections - 1 - step, sections - step) if 0 < p < sections]
            got = [
                lax.ppermute(back, ALL, hop_pairs(planes, size, by)) for by in (1, 0, -1)
            ]

    mine, theirs = call(
        wgrad_kernel,
        [VMEM] * 4,
        [out((GROUPS, WIN, CH), F32), out((GROUPS, WIN, CH), BF)],
        (pack, up1, down1, state),
        scratch=[pltpu.VMEM((9 * CH, CH), F32)],
        flops=1 << 28,
        moved=4 << 20,
    )
    received = lax.ppermute(theirs, "c", swap)
    (grads,) = call(grads_kernel, [SMEM, VMEM], [out(image, BF)], (order, state), moved=1 << 18)
    (both,) = call(
        pair_kernel,
        [VMEM] * 2,
        [out((GROUPS, WIN, CH), BF)],
        (mine, received),
        moved=3 << 20,
    )
    parts = lax.all_to_all(both, ("x", "z"), 0, 0)
    wgrad, bgrad = call(
        total_kernel,
        [VMEM],
        [out((PART, CH), F32), out((1, 4), F32)],
        (parts,),
        moved=1 << 20,
    )
    return grads.reshape(1, 2, 1, COLS, CH), wgrad[None], bgrad


def solution(mesh):
    fine = Mesh(mesh.devices.reshape(8, 4, 8, 2), ALL)
    placed = (
        P("y", None, SEC, None, None),
        P("y", SEC, None),
        P("y", None),
        P(None, SEC, None, None),
        P(SEC, None),
        P(SEC),
        P(),
    )
    return jax.shard_map(
        body,
        mesh=fine,
        in_specs=placed,
        out_specs=(P("y", None, SEC, None, None), P("y", SEC, None), P("y", SEC)),
        check_vma=False,
    )
```

```python
import jax
import jax.numpy as jnp
from jax import lax
from jax.experimental import pallas as pl
from jax.experimental.pallas import tpu as pltpu
from jax.sharding import Mesh
from jax.sharding import PartitionSpec as P

TILE = 16
COLS = 128
CH = 256
PART = 36
WIN = 40
GROUPS = 32
BF = jnp.bfloat16
F32 = jnp.float32
VMEM = pl.BlockSpec(memory_space=pltpu.VMEM)
SMEM = pl.BlockSpec(memory_space=pltpu.SMEM)
HBM = pl.BlockSpec(memory_space=pltpu.HBM)
ANY = pl.BlockSpec(memory_space=pl.ANY)
ALL = ("y", "x", "z", "c")
SEC = ("x", "z", "c")


def call(kernel, ins, outs, operands, aliases=None, scratch=(), flops=1, moved=1):
    return pl.pallas_call(
        kernel,
        out_shape=outs,
        in_specs=ins,
        out_specs=[VMEM] * len(outs),
        scratch_shapes=scratch,
        input_output_aliases=aliases or {},
        compiler_params=pltpu.CompilerParams(vmem_limit_bytes=24 << 20),
        cost_estimate=pl.CostEstimate(flops=flops, bytes_accessed=moved, transcendentals=0),
    )(*operands)


def out(shape, dtype):
    return jax.ShapeDtypeStruct(shape, dtype)


def from_left(x):
    return jnp.concatenate([jnp.zeros_like(x[:1]), x[:-1]], axis=0)


def from_right(x):
    return jnp.concatenate([x[1:], jnp.zeros_like(x[:1])], axis=0)


def wide_kernel(w, wide):
    core = lax.axis_index("c")
    rows = w[...].astype(F32)
    gap = jnp.zeros((WIN - PART, CH), F32)
    first = jnp.concatenate([rows, gap], axis=0)
    second = jnp.concatenate([gap, rows], axis=0)
    part = jnp.where(core == 0, first, second).astype(BF)
    for k in range(GROUPS):
        wide[k] = part


def pack_kernel(order, count, tiles, x, cot, send, keep, state):
    state[...] = jnp.zeros_like(state)
    core = lax.axis_index("c")
    most = tiles.shape[1]
    on = []
    for tile in range(COLS // TILE):
        live = jnp.int32(0)
        for k in range(most):
            live = live | ((tiles[0, k] == tile) & (k < count[0])).astype(jnp.int32)
        on.append(live.astype(F32))
    row = lax.broadcasted_iota(jnp.int32, (TILE, CH), 0)
    marks = jnp.zeros((TILE, CH), F32)
    for tile, value in enumerate(on):
        marks = jnp.where(row == tile, value, marks)
    for target, slot in ((keep, core), (send, 1 - core)):
        target[:COLS] = x[order[slot]]
        for tile, value in enumerate(on):
            rows = cot[slot, tile * TILE : (tile + 1) * TILE].astype(F32) * value
            target[COLS + tile * TILE : COLS + (tile + 1) * TILE] = rows.astype(BF)
        target[2 * COLS :] = marks.astype(BF)


def arrange_kernel(keep, got, block, both, first):
    core = lax.axis_index("c")

    def place(one, two):
        for j, rows in enumerate((one, two)):
            block[j * COLS : (j + 1) * COLS] = rows[:COLS]
            both[j * COLS : (j + 1) * COLS] = rows[:COLS]
            block[(2 + j) * COLS : (3 + j) * COLS] = rows[COLS : 2 * COLS]
            block[4 * COLS + j * TILE : 4 * COLS + (j + 1) * TILE] = rows[2 * COLS :]
        first[...] = one[:COLS]

    @pl.when(core == 0)
    def _():
        place(keep, got)

    @pl.when(core == 1)
    def _():
        place(got, keep)


def position():
    chip = lax.axis_index("x") * lax.axis_size("z") + lax.axis_index("z")
    odd = lax.axis_index("y") % 2 == 1
    return chip, odd


def keep_factor(chips):
    chip, odd = position()
    return jnp.where(odd & (chip == chips - 1), 0.0, 1.0).astype(BF)


def prep_kernel(mine, other, bias, block, before, after, second, deriv, weights, x6, mask):
    core = lax.axis_index("c")

    def assemble(even, odd):
        for k in range(GROUPS):
            base = 72 * k
            weights[base : base + 32] = even[k, 0:32]
            both = even[k, 32:40].astype(F32) + odd[k, 0:8].astype(F32)
            weights[base + 32 : base + 40] = both.astype(BF)
            weights[base + 40 : base + 72] = odd[k, 8:40]

    @pl.when(core == 0)
    def _():
        assemble(mine, other)

    @pl.when(core == 1)
    def _():
        assemble(other, mine)

    chip, odd = position()
    even = jnp.logical_not(odd)
    last = GROUPS - 1

    def rows(ref, j):
        return ref[j * COLS : (j + 1) * COLS]

    own0, own1 = rows(block, 0), rows(block, 1)
    next0, next1 = rows(after, 0), rows(after, 1)
    prev0, prev1 = rows(before, 0), rows(before, 1)
    zero = jnp.zeros((COLS, CH), BF)
    start = even & (chip == 0)
    end = even & (chip == last)
    cut0 = start | (odd & (chip == 0))
    cut5 = end | (odd & (chip == last - 1))
    x6[0] = jnp.where(cut0, zero, jnp.where(odd, prev1, prev0))
    x6[1] = jnp.where(start, zero, jnp.where(odd, own0, prev1))
    x6[2] = jnp.where(odd, own1, own0)
    x6[3] = jnp.where(odd, next0, own1)
    x6[4] = jnp.where(end, zero, jnp.where(odd, next1, next0))
    x6[5] = jnp.where(cut5, zero, jnp.where(odd, second[...], next1))

    own_marks = block[4 * COLS :].astype(F32)
    next_marks = after[4 * COLS :].astype(F32)
    for j in range(2):
        here = own_marks[j * TILE : (j + 1) * TILE]
        there = own_marks[TILE:] if j == 0 else next_marks[:TILE]
        marks = jnp.where(odd, there, here)
        for tile in range(COLS // TILE):
            mask[j * COLS + tile * TILE : j * COLS + (tile + 1) * TILE] = jnp.broadcast_to(
                marks[tile : tile + 1], (TILE, CH)
            )

    keep = keep_factor(GROUPS)
    lhs = [
        jnp.concatenate([x6[0], x6[1], x6[2] * keep, x6[3]], axis=0),
        jnp.concatenate([x6[1], x6[2], x6[3], x6[4]], axis=0),
        jnp.concatenate([x6[2], x6[3] * keep, x6[4], x6[5]], axis=0),
    ]
    shift = jnp.broadcast_to(bias[...], (COLS, CH))
    sums = []
    for b in range(3):
        total = None
        for a in range(3):
            tap = (3 * a + b) * CH
            term = jnp.dot(lhs[a], weights[tap : tap + CH], preferred_element_type=F32)
            total = term if total is None else total + term
        sums.append(total)
    for r in range(4):
        part = slice(r * COLS, (r + 1) * COLS)
        pre = from_left(sums[0][part]) + sums[1][part] + from_right(sums[2][part]) + shift
        sig = jax.nn.sigmoid(pre)
        value = sig * (1.0 + pre * (1.0 - sig))
        if r == 0:
            value = jnp.where(start, 0.0, value)
        if r == 3:
            value = jnp.where(end, 0.0, value)
        deriv[r] = value


def step_kernel(step, sections, mask, deriv, weights, low, high, state_in, *outs):
    state = outs[0]
    state[...] = state_in[...]

    @pl.when(lax.axis_index("y") == sections - 1 - step)
    def _():
        base = 2 * COLS if step == 0 else 0
        keep = keep_factor(GROUPS)
        gpre = []
        for r in range(4):
            at = base + (r % 2) * COLS
            upstream = (low if r < 2 else high)[at : at + COLS]
            gpre.append((upstream.astype(F32) * deriv[r]).astype(BF))
        state[0] = gpre[1]
        state[1] = gpre[2]
        lhs = [
            jnp.concatenate([gpre[2] * keep, gpre[3]], axis=0),
            jnp.concatenate([gpre[1], gpre[2]], axis=0),
            jnp.concatenate([gpre[0], gpre[1] * keep], axis=0),
        ]
        sums = []
        for b in range(3):
            total = None
            for a in range(3):
                tap = (3 * a + b) * CH
                term = lax.dot_general(
                    lhs[a],
                    weights[tap : tap + CH],
                    (((1,), (1,)), ((), ())),
                    preferred_element_type=F32,
                )
                total = term if total is None else total + term
            sums.append(total)
        for j in range(2):
            part = slice(j * COLS, (j + 1) * COLS)
            value = from_right(sums[0][part]) + sums[1][part] + from_left(sums[2][part])
            value = (value * mask[part]).astype(BF)
            state[2 + j] = value
            if len(outs) > 1:
                outs[1][part] = value


def grads_kernel(order, state, got, other, grads):
    core = lax.axis_index("c")
    _, odd = position()
    grads[order[1 - core]] = got[...]
    mine = jnp.where(core == 0, other[...], state[2])
    grads[order[core]] = jnp.where(odd, mine, state[2 + core])


def wgrad_kernel(x6, state, mine, theirs, send, spill, total):
    core = lax.axis_index("c")
    _, odd = position()
    send[...] = jnp.where(odd == (core == 1), state[3], state[2])
    spill[...] = state[3]
    keep = keep_factor(GROUPS)
    g = [state[j].astype(F32) for j in range(2)]
    shifted = [
        jnp.concatenate([from_right(g[0]), from_right(g[1])], axis=0).astype(BF),
        jnp.concatenate([state[0], state[1]], axis=0),
        jnp.concatenate([from_left(g[0]), from_left(g[1])], axis=0).astype(BF),
    ]
    lhs = [
        jnp.concatenate([x6[1], x6[2] * keep], axis=0),
        jnp.concatenate([x6[2], x6[3]], axis=0),
        jnp.concatenate([x6[3] * keep, x6[4]], axis=0),
    ]
    for a, x in enumerate(lhs):
        for b in range(3):
            tap = (3 * a + b) * CH
            total[tap : tap + CH] = lax.dot_general(
                x, shifted[b], (((0,), (0,)), ((), ())), preferred_element_type=F32
            )
    bias = jnp.sum(g[0] + g[1], axis=0, keepdims=True)
    high = bias.astype(BF).astype(F32)
    low = (bias - high).astype(BF).astype(F32)
    row = lax.broadcasted_iota(jnp.int32, (WIN, CH), 0)

    def window(which, start):
        at = jnp.where(which == 0, PART, 0)
        return total[pl.ds(pl.multiple_of(start, 8), WIN), :], at

    for k in range(GROUPS):
        value, at = window(core, 72 * k + 32 * core)
        value = jnp.where(row == at, bias, value)
        mine[k] = jnp.where(row == at + 1, 0.0, value)
        value, at = window(1 - core, 72 * k + 32 * (1 - core))
        value = jnp.where(row == at, high, value)
        theirs[k] = jnp.where(row == at + 1, low, value).astype(BF)


def pair_kernel(mine, got, both):
    core = lax.axis_index("c")
    row = lax.broadcasted_iota(jnp.int32, (WIN, CH), 0)
    at = jnp.where(core == 0, PART, 0)
    lead = mine[0] + got[0].astype(F32)
    here = (row == at) | (row == at + 1)
    bias = jnp.sum(jnp.where(here, lead, 0.0), axis=0, keepdims=True)
    high = bias.astype(BF).astype(F32)
    low = bias - high
    for k in range(GROUPS):
        value = mine[k] + got[k].astype(F32)
        value = jnp.where(row == at, high, value)
        both[k] = jnp.where(row == at + 1, low, value).astype(BF)


def total_kernel(parts, wgrad, bgrad):
    core = lax.axis_index("c")
    me = (lax.axis_index("x") * lax.axis_size("z") + lax.axis_index("z")) * 2 + core
    value = parts[0].astype(F32)
    for k in range(1, GROUPS):
        value = value + parts[k].astype(F32)
    wgrad[...] = jnp.where(core == 0, value[:PART], value[WIN - PART :])
    row = lax.broadcasted_iota(jnp.int32, (WIN, CH), 0)
    at = jnp.where(core == 0, PART, 0)
    here = (row == at) | (row == at + 1)
    bias = jnp.sum(jnp.where(here, value, 0.0), axis=0, keepdims=True)
    lane = lax.broadcasted_iota(jnp.int32, (1, CH), 1)
    spot = lax.broadcasted_iota(jnp.int32, (1, 4), 1)
    result = jnp.zeros((1, 4), F32)
    for j in range(4):
        one = jnp.sum(jnp.where(lane == 4 * me + j, bias, 0.0), axis=1, keepdims=True)
        result = jnp.where(spot == j, one, result)
    bgrad[...] = result


def chip_pairs(planes, by, down=0):
    return [
        (p * 64 + 2 * k + c, (p - down) * 64 + 2 * ((k + by) % GROUPS) + c)
        for p in planes
        for k in range(GROUPS)
        for c in range(2)
    ]


def return_pairs(sections):
    pairs = []
    for p in range(sections):
        for k in range(GROUPS):
            one, two = p * 64 + 2 * k, p * 64 + 2 * k + 1
            pairs.append((one, two))
            pairs.append((two, p * 64 + 2 * ((k + 1) % GROUPS)) if p % 2 else (two, one))
    return pairs


def body(saved_inputs, weights, biases, cotangent, tile_list, tile_count, order):
    sections = lax.axis_size("y")
    every = range(sections)
    odds = range(1, sections, 2)
    image = (2, COLS, CH)
    inputs = saved_inputs.reshape(image)
    cot = cotangent.reshape(image)

    (wide,) = call(
        wide_kernel, [VMEM], [out((GROUPS, WIN, CH), BF)], (weights[0],), moved=1 << 20
    )
    swap = [(0, 1), (1, 0)]
    mine = lax.all_to_all(wide, ("x", "z"), 0, 0)

    send, keep, state = call(
        pack_kernel,
        [SMEM] * 3 + [VMEM] * 2,
        [out((2 * COLS + TILE, CH), BF)] * 2 + [out((4, COLS, CH), BF)],
        (order, tile_count, tile_list, inputs, cot),
        flops=1 << 28,
        moved=3 << 20,
    )
    got = lax.ppermute(send, "c", swap)
    block, both, first = call(
        arrange_kernel,
        [VMEM] * 2,
        [
            out((4 * COLS + 2 * TILE, CH), BF),
            out((2 * COLS, CH), BF),
            out((COLS, CH), BF),
        ],
        (keep, got),
        flops=1 << 26,
        moved=1 << 20,
    )
    after = lax.ppermute(block, ALL, chip_pairs(every, -1))
    before = lax.ppermute(both, ALL, chip_pairs(every, 1))
    second = lax.ppermute(first, ALL, chip_pairs(odds, -2))
    mine, after, before, second = lax.optimization_barrier((mine, after, before, second))
    other = lax.ppermute(mine, "c", swap)

    deriv, wfull, x6, mask = call(
        prep_kernel,
        [VMEM] * 7,
        [
            out((4, COLS, CH), F32),
            out((9 * CH, CH), BF),
            out((6, COLS, CH), BF),
            out((2 * COLS, CH), F32),
        ],
        (mine, other, biases, block, before, after, second),
        flops=1 << 30,
        moved=4 << 20,
    )

    low, high = block, after
    for step in range(sections):
        live = step < sections - 1
        state, *back = call(
            lambda *refs, step=step: step_kernel(step, sections, *refs),
            [VMEM] * 6,
            [out((4, COLS, CH), BF)] + [out((2 * COLS, CH), BF)] * live,
            (mask, deriv, wfull, low, high, state),
            aliases={5: 0},
            flops=1 << 27,
            moved=2 << 20,
        )
        if live:
            plane = sections - 1 - step
            straight = lax.ppermute(back[0], ALL, chip_pairs([plane], 0, 1))
            if plane % 2:
                side = lax.ppermute(back[0], ALL, chip_pairs([plane], 1, 1))
                low, high = side, straight
            else:
                side = lax.ppermute(back[0], ALL, chip_pairs([plane], -1, 1))
                low, high = straight, side

    mine, theirs, send, spill = call(
        wgrad_kernel,
        [VMEM] * 2,
        [out((GROUPS, WIN, CH), F32), out((GROUPS, WIN, CH), BF)] + [out((COLS, CH), BF)] * 2,
        (x6, state),
        scratch=[pltpu.VMEM((9 * CH, CH), F32)],
        flops=1 << 28,
        moved=4 << 20,
    )
    received = lax.ppermute(theirs, "c", swap)
    got = lax.ppermute(send, ALL, return_pairs(sections))
    spilled = lax.ppermute(spill, ALL, chip_pairs(odds, 1))
    (grads,) = call(
        grads_kernel,
        [SMEM] + [VMEM] * 3,
        [out(image, BF)],
        (order, state, got, spilled),
        moved=1 << 18,
    )
    (both,) = call(
        pair_kernel,
        [VMEM] * 2,
        [out((GROUPS, WIN, CH), BF)],
        (mine, received),
        moved=3 << 20,
    )
    parts = lax.all_to_all(both, ("x", "z"), 0, 0)
    wgrad, bgrad = call(
        total_kernel,
        [VMEM],
        [out((PART, CH), F32), out((1, 4), F32)],
        (parts,),
        moved=1 << 20,
    )
    return grads.reshape(1, 2, 1, COLS, CH), wgrad[None], bgrad


def solution(mesh):
    fine = Mesh(mesh.devices.reshape(8, 4, 8, 2), ALL)
    placed = (
        P("y", None, SEC, None, None),
        P("y", SEC, None),
        P("y", None),
        P(None, SEC, None, None),
        P(SEC, None),
        P(SEC),
        P(),
    )
    return jax.shard_map(
        body,
        mesh=fine,
        in_specs=placed,
        out_specs=(P("y", None, SEC, None, None), P("y", SEC, None), P("y", SEC)),
        check_vma=False,
    )
```

```python
import jax
import jax.numpy as jnp
from jax import lax
from jax.experimental import pallas as pl
from jax.experimental.pallas import tpu as pltpu
from jax.sharding import Mesh
from jax.sharding import PartitionSpec as P

TILE = 16
COLS = 128
CH = 256
PART = 36
WIN = 40
GROUPS = 32
BF = jnp.bfloat16
F32 = jnp.float32
VMEM = pl.BlockSpec(memory_space=pltpu.VMEM)
SMEM = pl.BlockSpec(memory_space=pltpu.SMEM)
HBM = pl.BlockSpec(memory_space=pltpu.HBM)
ANY = pl.BlockSpec(memory_space=pl.ANY)
ALL = ("y", "x", "z", "c")
SEC = ("x", "z", "c")


def call(kernel, ins, outs, operands, aliases=None, scratch=(), flops=1, moved=1):
    return pl.pallas_call(
        kernel,
        out_shape=outs,
        in_specs=ins,
        out_specs=[VMEM] * len(outs),
        scratch_shapes=scratch,
        input_output_aliases=aliases or {},
        compiler_params=pltpu.CompilerParams(vmem_limit_bytes=24 << 20),
        cost_estimate=pl.CostEstimate(flops=flops, bytes_accessed=moved, transcendentals=0),
    )(*operands)


def out(shape, dtype):
    return jax.ShapeDtypeStruct(shape, dtype)


def from_left(x):
    return jnp.concatenate([jnp.zeros_like(x[:1]), x[:-1]], axis=0)


def from_right(x):
    return jnp.concatenate([x[1:], jnp.zeros_like(x[:1])], axis=0)


def wide_kernel(w, wide):
    core = lax.axis_index("c")
    rows = w[...].astype(F32)
    gap = jnp.zeros((WIN - PART, CH), F32)
    first = jnp.concatenate([rows, gap], axis=0)
    second = jnp.concatenate([gap, rows], axis=0)
    part = jnp.where(core == 0, first, second).astype(BF)
    for k in range(GROUPS):
        wide[k] = part


def pack_kernel(order, count, tiles, x, cot, send, keep, state):
    state[...] = jnp.zeros_like(state)
    core = lax.axis_index("c")
    most = tiles.shape[1]
    on = []
    for tile in range(COLS // TILE):
        live = jnp.int32(0)
        for k in range(most):
            live = live | ((tiles[0, k] == tile) & (k < count[0])).astype(jnp.int32)
        on.append(live.astype(F32))
    row = lax.broadcasted_iota(jnp.int32, (TILE, CH), 0)
    marks = jnp.zeros((TILE, CH), F32)
    for tile, value in enumerate(on):
        marks = jnp.where(row == tile, value, marks)
    for target, slot in ((keep, core), (send, 1 - core)):
        target[:COLS] = x[order[slot]]
        for tile, value in enumerate(on):
            rows = cot[slot, tile * TILE : (tile + 1) * TILE].astype(F32) * value
            target[COLS + tile * TILE : COLS + (tile + 1) * TILE] = rows.astype(BF)
        target[2 * COLS :] = marks.astype(BF)


def arrange_kernel(keep, got, block, up, down, first):
    core = lax.axis_index("c")

    def place(one, two):
        block[:COLS] = one[:COLS]
        block[COLS : 2 * COLS] = two[:COLS]
        block[2 * COLS : 3 * COLS] = one[COLS : 2 * COLS]
        block[3 * COLS : 4 * COLS] = two[COLS : 2 * COLS]
        block[4 * COLS : 4 * COLS + TILE] = one[2 * COLS :]
        block[4 * COLS + TILE :] = two[2 * COLS :]
        for target in (up, down):
            target[:COLS] = one[:COLS]
            target[COLS : 2 * COLS] = two[:COLS]
        down[2 * COLS : 3 * COLS] = one[COLS : 2 * COLS]
        down[3 * COLS : 4 * COLS] = two[COLS : 2 * COLS]
        down[4 * COLS :] = one[2 * COLS :]
        first[...] = one[:COLS]

    @pl.when(core == 0)
    def _():
        place(keep, got)

    @pl.when(core == 1)
    def _():
        place(got, keep)


def position():
    chip = lax.axis_index("x") * lax.axis_size("z") + lax.axis_index("z")
    shifted = lax.axis_index("y") % 2 == 1
    return chip, shifted


def keep_factor(chips):
    chip, shifted = position()
    return jnp.where(shifted & (chip == chips - 1), 0.0, 1.0).astype(BF)


def prep_kernel(mine, other, bias, block, before, after, second, deriv, weights, x6, mask):
    core = lax.axis_index("c")

    def assemble(even, odd):
        for k in range(GROUPS):
            base = 72 * k
            weights[base : base + 32] = even[k, 0:32]
            both = even[k, 32:40].astype(F32) + odd[k, 0:8].astype(F32)
            weights[base + 32 : base + 40] = both.astype(BF)
            weights[base + 40 : base + 72] = odd[k, 8:40]

    @pl.when(core == 0)
    def _():
        assemble(mine, other)

    @pl.when(core == 1)
    def _():
        assemble(other, mine)

    chip, shifted = position()
    aligned = jnp.logical_not(shifted)
    last = GROUPS - 1

    def rows(ref, j):
        return ref[j * COLS : (j + 1) * COLS]

    own0, own1 = rows(block, 0), rows(block, 1)
    next0, next1 = rows(after, 0), rows(after, 1)
    prev0, prev1 = rows(before, 0), rows(before, 1)
    zero = jnp.zeros((COLS, CH), BF)
    start = aligned & (chip == 0)
    end = aligned & (chip == last)
    cut0 = start | (shifted & (chip == 0))
    cut5 = end | (shifted & (chip == last - 1))
    x6[0] = jnp.where(cut0, zero, jnp.where(shifted, prev1, prev0))
    x6[1] = jnp.where(start, zero, jnp.where(shifted, own0, prev1))
    x6[2] = jnp.where(shifted, own1, own0)
    x6[3] = jnp.where(shifted, next0, own1)
    x6[4] = jnp.where(end, zero, jnp.where(shifted, next1, next0))
    x6[5] = jnp.where(cut5, zero, jnp.where(shifted, second[...], next1))

    own_marks = block[4 * COLS :].astype(F32)
    next_marks = after[4 * COLS :].astype(F32)
    for j in range(2):
        here = own_marks[j * TILE : (j + 1) * TILE]
        there = own_marks[TILE:] if j == 0 else next_marks
        marks = jnp.where(shifted, there, here)
        for tile in range(COLS // TILE):
            mask[j * COLS + tile * TILE : j * COLS + (tile + 1) * TILE] = jnp.broadcast_to(
                marks[tile : tile + 1], (TILE, CH)
            )

    keep = keep_factor(GROUPS)
    lhs = [
        jnp.concatenate([x6[0], x6[1], x6[2] * keep, x6[3]], axis=0),
        jnp.concatenate([x6[1], x6[2], x6[3], x6[4]], axis=0),
        jnp.concatenate([x6[2], x6[3] * keep, x6[4], x6[5]], axis=0),
    ]
    shift = jnp.broadcast_to(bias[...], (COLS, CH))
    sums = []
    for b in range(3):
        total = None
        for a in range(3):
            tap = (3 * a + b) * CH
            term = jnp.dot(lhs[a], weights[tap : tap + CH], preferred_element_type=F32)
            total = term if total is None else total + term
        sums.append(total)
    for r in range(4):
        part = slice(r * COLS, (r + 1) * COLS)
        pre = from_left(sums[0][part]) + sums[1][part] + from_right(sums[2][part]) + shift
        sig = jax.nn.sigmoid(pre)
        value = sig * (1.0 + pre * (1.0 - sig))
        if r == 0:
            value = jnp.where(start, 0.0, value)
        if r == 3:
            value = jnp.where(end, 0.0, value)
        deriv[r] = value


def step_kernel(step, sections, mask, deriv, weights, *refs):
    arrived, state_in, outs = refs[:2], refs[2], refs[3:]
    state = outs[0]
    state[...] = state_in[...]

    @pl.when(lax.axis_index("y") == sections - 1 - step)
    def _():
        keep = keep_factor(GROUPS)
        if step == 0:
            block, after = arrived
            sources = [(block, 2), (block, 3), (after, 2), (after, 3)]
        else:
            straight, side = arrived
            low, high = (side, straight) if step % 2 else (straight, side)
            sources = [(low, 0), (low, 1), (high, 0), (high, 1)]
        gpre = []
        for r, (ref, at) in enumerate(sources):
            upstream = ref[at * COLS : (at + 1) * COLS]
            gpre.append((upstream.astype(F32) * deriv[r]).astype(BF))
        state[0] = gpre[1]
        state[1] = gpre[2]
        lhs = [
            jnp.concatenate([gpre[2] * keep, gpre[3]], axis=0),
            jnp.concatenate([gpre[1], gpre[2]], axis=0),
            jnp.concatenate([gpre[0], gpre[1] * keep], axis=0),
        ]
        sums = []
        for b in range(3):
            total = None
            for a in range(3):
                tap = (3 * a + b) * CH
                term = lax.dot_general(
                    lhs[a],
                    weights[tap : tap + CH],
                    (((1,), (1,)), ((), ())),
                    preferred_element_type=F32,
                )
                total = term if total is None else total + term
            sums.append(total)
        for j in range(2):
            part = slice(j * COLS, (j + 1) * COLS)
            value = from_right(sums[0][part]) + sums[1][part] + from_left(sums[2][part])
            value = (value * mask[part]).astype(BF)
            state[2 + j] = value
            if len(outs) > 1:
                outs[1][part] = value


def grads_kernel(order, state, got, other, grads):
    core = lax.axis_index("c")
    _, shifted = position()
    grads[order[1 - core]] = got[...]
    mine = jnp.where(core == 0, other[...], state[2])
    grads[order[core]] = jnp.where(shifted, mine, state[2 + core])


def wgrad_kernel(x6, state, mine, theirs, send, spill, total):
    core = lax.axis_index("c")
    _, shifted = position()
    send[...] = jnp.where(shifted == (core == 1), state[3], state[2])
    spill[...] = state[3]
    keep = keep_factor(GROUPS)
    g = [state[j].astype(F32) for j in range(2)]
    moved = [
        jnp.concatenate([from_right(g[0]), from_right(g[1])], axis=0).astype(BF),
        jnp.concatenate([state[0], state[1]], axis=0),
        jnp.concatenate([from_left(g[0]), from_left(g[1])], axis=0).astype(BF),
    ]
    lhs = [
        jnp.concatenate([x6[1], x6[2] * keep], axis=0),
        jnp.concatenate([x6[2], x6[3]], axis=0),
        jnp.concatenate([x6[3] * keep, x6[4]], axis=0),
    ]
    for a, x in enumerate(lhs):
        for b in range(3):
            tap = (3 * a + b) * CH
            total[tap : tap + CH] = lax.dot_general(
                x, moved[b], (((0,), (0,)), ((), ())), preferred_element_type=F32
            )
    bias = jnp.sum(g[0] + g[1], axis=0, keepdims=True)
    high = bias.astype(BF).astype(F32)
    low = (bias - high).astype(BF).astype(F32)
    row = lax.broadcasted_iota(jnp.int32, (WIN, CH), 0)

    def window(which, start):
        at = jnp.where(which == 0, PART, 0)
        return total[pl.ds(pl.multiple_of(start, 8), WIN), :], at

    for k in range(GROUPS):
        value, at = window(core, 72 * k + 32 * core)
        value = jnp.where(row == at, bias, value)
        mine[k] = jnp.where(row == at + 1, 0.0, value)
        value, at = window(1 - core, 72 * k + 32 * (1 - core))
        value = jnp.where(row == at, high, value)
        theirs[k] = jnp.where(row == at + 1, low, value).astype(BF)


def pair_kernel(mine, got, both):
    core = lax.axis_index("c")
    row = lax.broadcasted_iota(jnp.int32, (WIN, CH), 0)
    at = jnp.where(core == 0, PART, 0)
    lead = mine[0] + got[0].astype(F32)
    here = (row == at) | (row == at + 1)
    bias = jnp.sum(jnp.where(here, lead, 0.0), axis=0, keepdims=True)
    high = bias.astype(BF).astype(F32)
    low = bias - high
    for k in range(GROUPS):
        value = mine[k] + got[k].astype(F32)
        value = jnp.where(row == at, high, value)
        both[k] = jnp.where(row == at + 1, low, value).astype(BF)


def total_kernel(parts, wgrad, bgrad):
    core = lax.axis_index("c")
    me = (lax.axis_index("x") * lax.axis_size("z") + lax.axis_index("z")) * 2 + core
    value = parts[0].astype(F32)
    for k in range(1, GROUPS):
        value = value + parts[k].astype(F32)
    result = jnp.where(core == 0, value[:PART], value[WIN - PART :])
    half = CH // 2
    for j in range(2):
        wgrad[pl.ds(j, PART, stride=2), :] = result[:, j * half : (j + 1) * half]
    row = lax.broadcasted_iota(jnp.int32, (WIN, CH), 0)
    at = jnp.where(core == 0, PART, 0)
    here = (row == at) | (row == at + 1)
    bias = jnp.sum(jnp.where(here, value, 0.0), axis=0, keepdims=True)
    lane = lax.broadcasted_iota(jnp.int32, (1, CH), 1)
    spot = lax.broadcasted_iota(jnp.int32, (1, 4), 1)
    result = jnp.zeros((1, 4), F32)
    for j in range(4):
        one = jnp.sum(jnp.where(lane == 4 * me + j, bias, 0.0), axis=1, keepdims=True)
        result = jnp.where(spot == j, one, result)
    bgrad[...] = result


def chip_pairs(planes, by, down=0):
    return [
        (p * 64 + 2 * k + c, (p - down) * 64 + 2 * ((k + by) % GROUPS) + c)
        for p in planes
        for k in range(GROUPS)
        for c in range(2)
    ]


def return_pairs(sections):
    pairs = []
    for p in range(sections):
        for k in range(GROUPS):
            one, two = p * 64 + 2 * k, p * 64 + 2 * k + 1
            pairs.append((one, two))
            pairs.append((two, p * 64 + 2 * ((k + 1) % GROUPS)) if p % 2 else (two, one))
    return pairs


def body(saved_inputs, weights, biases, cotangent, tile_list, tile_count, order):
    sections = lax.axis_size("y")
    every = range(sections)
    shifts = range(1, sections, 2)
    image = (2, COLS, CH)
    inputs = saved_inputs.reshape(image)
    cot = cotangent.reshape(image)

    (wide,) = call(
        wide_kernel, [VMEM], [out((GROUPS, WIN, CH), BF)], (weights[0],), moved=1 << 20
    )
    swap = [(0, 1), (1, 0)]
    mine = lax.all_to_all(wide, ("x", "z"), 0, 0)

    send, keep, state = call(
        pack_kernel,
        [SMEM] * 3 + [VMEM] * 2,
        [out((2 * COLS + TILE, CH), BF)] * 2 + [out((4, COLS, CH), BF)],
        (order, tile_count, tile_list, inputs, cot),
        flops=1 << 28,
        moved=3 << 20,
    )
    got = lax.ppermute(send, "c", swap)
    block, up, down, first = call(
        arrange_kernel,
        [VMEM] * 2,
        [
            out((4 * COLS + 2 * TILE, CH), BF),
            out((2 * COLS, CH), BF),
            out((4 * COLS + TILE, CH), BF),
            out((COLS, CH), BF),
        ],
        (keep, got),
        flops=1 << 26,
        moved=1 << 20,
    )
    after = lax.ppermute(down, ALL, chip_pairs(every, -1))
    before = lax.ppermute(up, ALL, chip_pairs(every, 1))
    second = lax.ppermute(first, ALL, chip_pairs(shifts, -2))
    mine, after, before, second = lax.optimization_barrier((mine, after, before, second))
    other = lax.ppermute(mine, "c", swap)

    deriv, wfull, x6, mask = call(
        prep_kernel,
        [VMEM] * 7,
        [
            out((4, COLS, CH), F32),
            out((9 * CH, CH), BF),
            out((6, COLS, CH), BF),
            out((2 * COLS, CH), F32),
        ],
        (mine, other, biases, block, before, after, second),
        flops=1 << 30,
        moved=4 << 20,
    )

    arrived = [block, after]
    for step in range(sections):
        live = step < sections - 1
        state, *back = call(
            lambda *refs, step=step: step_kernel(step, sections, *refs),
            [VMEM] * (4 + len(arrived)),
            [out((4, COLS, CH), BF)] + [out((2 * COLS, CH), BF)] * live,
            (mask, deriv, wfull, *arrived, state),
            aliases={3 + len(arrived): 0},
            flops=1 << 27,
            moved=2 << 20,
        )
        if live:
            plane = sections - 1 - step
            straight = lax.ppermute(back[0], ALL, chip_pairs([plane], 0, 1))
            side = lax.ppermute(back[0], ALL, chip_pairs([plane], 1 if plane % 2 else -1, 1))
            arrived = [straight, side]

    mine, theirs, send, spill = call(
        wgrad_kernel,
        [VMEM] * 2,
        [out((GROUPS, WIN, CH), F32), out((GROUPS, WIN, CH), BF)] + [out((COLS, CH), BF)] * 2,
        (x6, state),
        scratch=[pltpu.VMEM((9 * CH, CH), F32)],
        flops=1 << 28,
        moved=4 << 20,
    )
    received = lax.ppermute(theirs, "c", swap)
    got = lax.ppermute(send, ALL, return_pairs(sections))
    spilled = lax.ppermute(spill, ALL, chip_pairs(shifts, 1))
    (grads,) = call(
        grads_kernel,
        [SMEM] + [VMEM] * 3,
        [out(image, BF)],
        (order, state, got, spilled),
        moved=1 << 18,
    )
    (both,) = call(
        pair_kernel,
        [VMEM] * 2,
        [out((GROUPS, WIN, CH), BF)],
        (mine, received),
        moved=3 << 20,
    )
    parts = lax.all_to_all(both, ("x", "z"), 0, 0)
    wgrad, bgrad = call(
        total_kernel,
        [VMEM],
        [out((2 * PART, CH // 2), F32), out((1, 4), F32)],
        (parts,),
        moved=1 << 20,
    )
    return grads.reshape(1, 2, 1, COLS, CH), wgrad.reshape(1, PART, CH), bgrad


def solution(mesh):
    fine = Mesh(mesh.devices.reshape(8, 4, 8, 2), ALL)
    placed = (
        P("y", None, SEC, None, None),
        P("y", SEC, None),
        P("y", None),
        P(None, SEC, None, None),
        P(SEC, None),
        P(SEC),
        P(),
    )
    return jax.shard_map(
        body,
        mesh=fine,
        in_specs=placed,
        out_specs=(P("y", None, SEC, None, None), P("y", SEC, None), P("y", SEC)),
        check_vma=False,
    )
```

```python
import jax
import jax.numpy as jnp
from jax import lax
from jax.experimental import pallas as pl
from jax.experimental.pallas import tpu as pltpu
from jax.sharding import Mesh
from jax.sharding import PartitionSpec as P

TILE = 16
COLS = 128
CH = 256
PART = 36
WIN = 40
GROUPS = 32
BF = jnp.bfloat16
F32 = jnp.float32
VMEM = pl.BlockSpec(memory_space=pltpu.VMEM)
SMEM = pl.BlockSpec(memory_space=pltpu.SMEM)
HBM = pl.BlockSpec(memory_space=pltpu.HBM)
ANY = pl.BlockSpec(memory_space=pl.ANY)
ALL = ("y", "x", "z", "c")
SEC = ("x", "z", "c")


def call(kernel, ins, outs, operands, aliases=None, scratch=(), flops=1, moved=1):
    return pl.pallas_call(
        kernel,
        out_shape=outs,
        in_specs=ins,
        out_specs=[VMEM] * len(outs),
        scratch_shapes=scratch,
        input_output_aliases=aliases or {},
        compiler_params=pltpu.CompilerParams(vmem_limit_bytes=24 << 20),
        cost_estimate=pl.CostEstimate(flops=flops, bytes_accessed=moved, transcendentals=0),
    )(*operands)


def out(shape, dtype):
    return jax.ShapeDtypeStruct(shape, dtype)


def from_left(x):
    return jnp.concatenate([jnp.zeros_like(x[:1]), x[:-1]], axis=0)


def from_right(x):
    return jnp.concatenate([x[1:], jnp.zeros_like(x[:1])], axis=0)


def wide_kernel(w, wide):
    core = lax.axis_index("c")
    rows = w[...].astype(F32)
    gap = jnp.zeros((WIN - PART, CH), F32)
    first = jnp.concatenate([rows, gap], axis=0)
    second = jnp.concatenate([gap, rows], axis=0)
    part = jnp.where(core == 0, first, second).astype(BF)
    for k in range(GROUPS):
        wide[k] = part


def pack_kernel(order, count, tiles, x, cot, send, keep, state):
    state[...] = jnp.zeros_like(state)
    core = lax.axis_index("c")
    most = tiles.shape[1]
    on = []
    for tile in range(COLS // TILE):
        live = jnp.int32(0)
        for k in range(most):
            live = live | ((tiles[0, k] == tile) & (k < count[0])).astype(jnp.int32)
        on.append(live.astype(F32))
    row = lax.broadcasted_iota(jnp.int32, (TILE, CH), 0)
    marks = jnp.zeros((TILE, CH), F32)
    for tile, value in enumerate(on):
        marks = jnp.where(row == tile, value, marks)
    for target, slot in ((keep, core), (send, 1 - core)):
        target[:COLS] = x[order[slot]]
        for tile, value in enumerate(on):
            rows = cot[slot, tile * TILE : (tile + 1) * TILE].astype(F32) * value
            target[COLS + tile * TILE : COLS + (tile + 1) * TILE] = rows.astype(BF)
        target[2 * COLS :] = marks.astype(BF)


def arrange_kernel(keep, got, block, up, down, first):
    core = lax.axis_index("c")

    def place(one, two):
        block[:COLS] = one[:COLS]
        block[COLS : 2 * COLS] = two[:COLS]
        block[2 * COLS : 3 * COLS] = one[COLS : 2 * COLS]
        block[3 * COLS : 4 * COLS] = two[COLS : 2 * COLS]
        block[4 * COLS : 4 * COLS + TILE] = one[2 * COLS :]
        block[4 * COLS + TILE :] = two[2 * COLS :]
        for target in (up, down):
            target[:COLS] = one[:COLS]
            target[COLS : 2 * COLS] = two[:COLS]
        down[2 * COLS : 3 * COLS] = one[COLS : 2 * COLS]
        down[3 * COLS : 4 * COLS] = two[COLS : 2 * COLS]
        down[4 * COLS :] = one[2 * COLS :]
        first[...] = one[:COLS]

    @pl.when(core == 0)
    def _():
        place(keep, got)

    @pl.when(core == 1)
    def _():
        place(got, keep)


def position():
    chip = lax.axis_index("x") * lax.axis_size("z") + lax.axis_index("z")
    shifted = lax.axis_index("y") % 2 == 1
    return chip, shifted


def keep_factor(chips):
    chip, shifted = position()
    return jnp.where(shifted & (chip == chips - 1), 0.0, 1.0).astype(BF)


def prep_kernel(mine, other, bias, block, before, after, second, deriv, weights, x4, mask, x6):
    core = lax.axis_index("c")

    def assemble(even, odd):
        for k in range(GROUPS):
            base = 72 * k
            weights[base : base + 32] = even[k, 0:32]
            both = even[k, 32:40].astype(F32) + odd[k, 0:8].astype(F32)
            weights[base + 32 : base + 40] = both.astype(BF)
            weights[base + 40 : base + 72] = odd[k, 8:40]

    @pl.when(core == 0)
    def _():
        assemble(mine, other)

    @pl.when(core == 1)
    def _():
        assemble(other, mine)

    chip, shifted = position()
    aligned = jnp.logical_not(shifted)
    last = GROUPS - 1

    def rows(ref, j):
        return ref[j * COLS : (j + 1) * COLS]

    own0, own1 = rows(block, 0), rows(block, 1)
    next0, next1 = rows(after, 0), rows(after, 1)
    prev0, prev1 = rows(before, 0), rows(before, 1)
    zero = jnp.zeros((COLS, CH), BF)
    start = aligned & (chip == 0)
    end = aligned & (chip == last)
    cut0 = start | (shifted & (chip == 0))
    cut5 = end | (shifted & (chip == last - 1))
    x6[0] = jnp.where(cut0, zero, jnp.where(shifted, prev1, prev0))
    x6[1] = jnp.where(start, zero, jnp.where(shifted, own0, prev1))
    x6[2] = jnp.where(shifted, own1, own0)
    x6[3] = jnp.where(shifted, next0, own1)
    x6[4] = jnp.where(end, zero, jnp.where(shifted, next1, next0))
    x6[5] = jnp.where(cut5, zero, jnp.where(shifted, second[...], next1))

    own_marks = block[4 * COLS :].astype(F32)
    next_marks = after[4 * COLS :].astype(F32)
    for j in range(2):
        here = own_marks[j * TILE : (j + 1) * TILE]
        there = own_marks[TILE:] if j == 0 else next_marks
        marks = jnp.where(shifted, there, here)
        for tile in range(COLS // TILE):
            mask[j * COLS + tile * TILE : j * COLS + (tile + 1) * TILE] = jnp.broadcast_to(
                marks[tile : tile + 1], (TILE, CH)
            )

    for j in range(4):
        x4[j] = x6[1 + j]
    keep = keep_factor(GROUPS)
    lhs = [
        jnp.concatenate([x6[0], x6[1], x6[2] * keep, x6[3]], axis=0),
        jnp.concatenate([x6[1], x6[2], x6[3], x6[4]], axis=0),
        jnp.concatenate([x6[2], x6[3] * keep, x6[4], x6[5]], axis=0),
    ]
    shift = jnp.broadcast_to(bias[...], (COLS, CH))
    sums = []
    for b in range(3):
        total = None
        for a in range(3):
            tap = (3 * a + b) * CH
            term = jnp.dot(lhs[a], weights[tap : tap + CH], preferred_element_type=F32)
            total = term if total is None else total + term
        sums.append(total)
    for r in range(4):
        part = slice(r * COLS, (r + 1) * COLS)
        pre = from_left(sums[0][part]) + sums[1][part] + from_right(sums[2][part]) + shift
        sig = jax.nn.sigmoid(pre)
        value = sig * (1.0 + pre * (1.0 - sig))
        if r == 0:
            value = jnp.where(start, 0.0, value)
        if r == 3:
            value = jnp.where(end, 0.0, value)
        deriv[r] = value


def step_kernel(step, sections, mask, deriv, weights, *refs):
    arrived, state_in, outs = refs[:2], refs[2], refs[3:]
    state = outs[0]
    state[...] = state_in[...]

    @pl.when(lax.axis_index("y") == sections - 1 - step)
    def _():
        keep = keep_factor(GROUPS)
        if step == 0:
            block, after = arrived
            sources = [(block, 2), (block, 3), (after, 2), (after, 3)]
        else:
            straight, side = arrived
            low, high = (side, straight) if step % 2 else (straight, side)
            sources = [(low, 0), (low, 1), (high, 0), (high, 1)]
        gpre = []
        for r, (ref, at) in enumerate(sources):
            upstream = ref[at * COLS : (at + 1) * COLS]
            gpre.append((upstream.astype(F32) * deriv[r]).astype(BF))
        state[0] = gpre[1]
        state[1] = gpre[2]
        lhs = [
            jnp.concatenate([gpre[2] * keep, gpre[3]], axis=0),
            jnp.concatenate([gpre[1], gpre[2]], axis=0),
            jnp.concatenate([gpre[0], gpre[1] * keep], axis=0),
        ]
        sums = []
        for b in range(3):
            total = None
            for a in range(3):
                tap = (3 * a + b) * CH
                term = lax.dot_general(
                    lhs[a],
                    weights[tap : tap + CH],
                    (((1,), (1,)), ((), ())),
                    preferred_element_type=F32,
                )
                total = term if total is None else total + term
            sums.append(total)
        for j in range(2):
            part = slice(j * COLS, (j + 1) * COLS)
            value = from_right(sums[0][part]) + sums[1][part] + from_left(sums[2][part])
            value = (value * mask[part]).astype(BF)
            state[2 + j] = value
            if step < sections - 1:
                outs[1][part] = value

    if step == sections - 1:
        for j in range(2):
            outs[1][j * COLS : (j + 1) * COLS] = state[j]


def grads_kernel(order, state, got, other, grads):
    core = lax.axis_index("c")
    _, shifted = position()
    grads[order[1 - core]] = got[...]
    mine = jnp.where(core == 0, other[...], state[2])
    grads[order[core]] = jnp.where(shifted, mine, state[2 + core])


def wgrad_kernel(x_own, x_other, state, g_other, parts, send, spill, total):
    core = lax.axis_index("c")
    _, shifted = position()
    send[...] = jnp.where(shifted == (core == 1), state[3], state[2])
    spill[...] = state[3]
    keep = keep_factor(GROUPS)
    rows = [state[0], state[1], g_other[:COLS], g_other[COLS:]]
    g = [value.astype(F32) for value in rows]
    moved = [
        jnp.concatenate([from_right(value) for value in g], axis=0).astype(BF),
        jnp.concatenate(rows, axis=0),
        jnp.concatenate([from_left(value) for value in g], axis=0).astype(BF),
    ]
    pairs = (x_own, x_other)
    lhs = [
        jnp.concatenate([v for x in pairs for v in (x[0], x[1] * keep)], axis=0),
        jnp.concatenate([v for x in pairs for v in (x[1], x[2])], axis=0),
        jnp.concatenate([v for x in pairs for v in (x[2] * keep, x[3])], axis=0),
    ]
    for a, x in enumerate(lhs):
        for b in range(3):
            tap = (3 * a + b) * CH
            total[tap : tap + CH] = lax.dot_general(
                x, moved[b], (((0,), (0,)), ((), ())), preferred_element_type=F32
            )
    bias = jnp.sum((g[0] + g[1]) + (g[2] + g[3]), axis=0, keepdims=True)
    high = bias.astype(BF).astype(F32)
    low = bias - high
    row = lax.broadcasted_iota(jnp.int32, (WIN, CH), 0)
    at = jnp.where(core == 0, PART, 0)
    for k in range(GROUPS):
        value = total[pl.ds(pl.multiple_of(72 * k + 32 * core, 8), WIN), :]
        value = jnp.where(row == at, high, value)
        parts[k] = jnp.where(row == at + 1, low, value).astype(BF)


def total_kernel(parts, wgrad, bgrad):
    core = lax.axis_index("c")
    me = (lax.axis_index("x") * lax.axis_size("z") + lax.axis_index("z")) * 2 + core
    value = parts[0].astype(F32)
    for k in range(1, GROUPS):
        value = value + parts[k].astype(F32)
    result = jnp.where(core == 0, value[:PART], value[WIN - PART :])
    half = CH // 2
    for j in range(2):
        wgrad[pl.ds(j, PART, stride=2), :] = result[:, j * half : (j + 1) * half]
    row = lax.broadcasted_iota(jnp.int32, (WIN, CH), 0)
    at = jnp.where(core == 0, PART, 0)
    here = (row == at) | (row == at + 1)
    bias = jnp.sum(jnp.where(here, value, 0.0), axis=0, keepdims=True)
    lane = lax.broadcasted_iota(jnp.int32, (1, CH), 1)
    spot = lax.broadcasted_iota(jnp.int32, (1, 4), 1)
    result = jnp.zeros((1, 4), F32)
    for j in range(4):
        one = jnp.sum(jnp.where(lane == 4 * me + j, bias, 0.0), axis=1, keepdims=True)
        result = jnp.where(spot == j, one, result)
    bgrad[...] = result


def chip_pairs(planes, by, down=0):
    return [
        (p * 64 + 2 * k + c, (p - down) * 64 + 2 * ((k + by) % GROUPS) + c)
        for p in planes
        for k in range(GROUPS)
        for c in range(2)
    ]


def return_pairs(sections):
    pairs = []
    for p in range(sections):
        for k in range(GROUPS):
            one, two = p * 64 + 2 * k, p * 64 + 2 * k + 1
            pairs.append((one, two))
            pairs.append((two, p * 64 + 2 * ((k + 1) % GROUPS)) if p % 2 else (two, one))
    return pairs


def body(saved_inputs, weights, biases, cotangent, tile_list, tile_count, order):
    sections = lax.axis_size("y")
    every = range(sections)
    shifts = range(1, sections, 2)
    image = (2, COLS, CH)
    inputs = saved_inputs.reshape(image)
    cot = cotangent.reshape(image)

    (wide,) = call(
        wide_kernel, [VMEM], [out((GROUPS, WIN, CH), BF)], (weights[0],), moved=1 << 20
    )
    swap = [(0, 1), (1, 0)]
    mine = lax.all_to_all(wide, ("x", "z"), 0, 0)

    send, keep, state = call(
        pack_kernel,
        [SMEM] * 3 + [VMEM] * 2,
        [out((2 * COLS + TILE, CH), BF)] * 2 + [out((4, COLS, CH), BF)],
        (order, tile_count, tile_list, inputs, cot),
        flops=1 << 28,
        moved=3 << 20,
    )
    got = lax.ppermute(send, "c", swap)
    block, up, down, first = call(
        arrange_kernel,
        [VMEM] * 2,
        [
            out((4 * COLS + 2 * TILE, CH), BF),
            out((2 * COLS, CH), BF),
            out((4 * COLS + TILE, CH), BF),
            out((COLS, CH), BF),
        ],
        (keep, got),
        flops=1 << 26,
        moved=1 << 20,
    )
    after = lax.ppermute(down, ALL, chip_pairs(every, -1))
    before = lax.ppermute(up, ALL, chip_pairs(every, 1))
    second = lax.ppermute(first, ALL, chip_pairs(shifts, -2))
    mine, after, before, second = lax.optimization_barrier((mine, after, before, second))
    other = lax.ppermute(mine, "c", swap)

    deriv, wfull, x4, mask = call(
        prep_kernel,
        [VMEM] * 7,
        [
            out((4, COLS, CH), F32),
            out((9 * CH, CH), BF),
            out((4, COLS, CH), BF),
            out((2 * COLS, CH), F32),
        ],
        (mine, other, biases, block, before, after, second),
        scratch=[pltpu.VMEM((6, COLS, CH), BF)],
        flops=1 << 30,
        moved=4 << 20,
    )

    arrived = [block, after]
    for step in range(sections):
        live = step < sections - 1
        state, back = call(
            lambda *refs, step=step: step_kernel(step, sections, *refs),
            [VMEM] * (4 + len(arrived)),
            [out((4, COLS, CH), BF), out((2 * COLS, CH), BF)],
            (mask, deriv, wfull, *arrived, state),
            aliases={3 + len(arrived): 0},
            flops=1 << 27,
            moved=2 << 20,
        )
        if live:
            plane = sections - 1 - step
            straight = lax.ppermute(back, ALL, chip_pairs([plane], 0, 1))
            side = lax.ppermute(back, ALL, chip_pairs([plane], 1 if plane % 2 else -1, 1))
            arrived = [straight, side]
        if step == 2:
            late, _ = lax.optimization_barrier((x4, back))
            x_other = lax.ppermute(late, "c", swap)

    g_other = lax.ppermute(back, "c", swap)
    both, send, spill = call(
        wgrad_kernel,
        [VMEM] * 4,
        [out((GROUPS, WIN, CH), BF)] + [out((COLS, CH), BF)] * 2,
        (x4, x_other, state, g_other),
        scratch=[pltpu.VMEM((9 * CH, CH), F32)],
        flops=1 << 28,
        moved=4 << 20,
    )
    got = lax.ppermute(send, ALL, return_pairs(sections))
    spilled = lax.ppermute(spill, ALL, chip_pairs(shifts, 1))
    (grads,) = call(
        grads_kernel,
        [SMEM] + [VMEM] * 3,
        [out(image, BF)],
        (order, state, got, spilled),
        moved=1 << 18,
    )
    parts = lax.all_to_all(both, ("x", "z"), 0, 0)
    wgrad, bgrad = call(
        total_kernel,
        [VMEM],
        [out((2 * PART, CH // 2), F32), out((1, 4), F32)],
        (parts,),
        moved=1 << 20,
    )
    return grads.reshape(1, 2, 1, COLS, CH), wgrad.reshape(1, PART, CH), bgrad


def solution(mesh):
    fine = Mesh(mesh.devices.reshape(8, 4, 8, 2), ALL)
    placed = (
        P("y", None, SEC, None, None),
        P("y", SEC, None),
        P("y", None),
        P(None, SEC, None, None),
        P(SEC, None),
        P(SEC),
        P(),
    )
    return jax.shard_map(
        body,
        mesh=fine,
        in_specs=placed,
        out_specs=(P("y", None, SEC, None, None), P("y", SEC, None), P("y", SEC)),
        check_vma=False,
    )
```

```python
import jax
import jax.numpy as jnp
from jax import lax
from jax.experimental import pallas as pl
from jax.experimental.pallas import tpu as pltpu
from jax.sharding import Mesh
from jax.sharding import PartitionSpec as P

TILE = 16
COLS = 128
CH = 256
PART = 36
WIN = 40
GROUPS = 32
BF = jnp.bfloat16
F32 = jnp.float32
VMEM = pl.BlockSpec(memory_space=pltpu.VMEM)
SMEM = pl.BlockSpec(memory_space=pltpu.SMEM)
HBM = pl.BlockSpec(memory_space=pltpu.HBM)
ANY = pl.BlockSpec(memory_space=pl.ANY)
ALL = ("y", "x", "z", "c")
SEC = ("x", "z", "c")


def call(kernel, ins, outs, operands, aliases=None, scratch=(), flops=1, moved=1):
    return pl.pallas_call(
        kernel,
        out_shape=outs,
        in_specs=ins,
        out_specs=[VMEM] * len(outs),
        scratch_shapes=scratch,
        input_output_aliases=aliases or {},
        compiler_params=pltpu.CompilerParams(vmem_limit_bytes=24 << 20),
        cost_estimate=pl.CostEstimate(flops=flops, bytes_accessed=moved, transcendentals=0),
    )(*operands)


def out(shape, dtype):
    return jax.ShapeDtypeStruct(shape, dtype)


def from_left(x):
    return jnp.concatenate([jnp.zeros_like(x[:1]), x[:-1]], axis=0)


def from_right(x):
    return jnp.concatenate([x[1:], jnp.zeros_like(x[:1])], axis=0)


def wide_kernel(w, wide):
    core = lax.axis_index("c")
    rows = w[...].astype(F32)
    gap = jnp.zeros((WIN - PART, CH), F32)
    first = jnp.concatenate([rows, gap], axis=0)
    second = jnp.concatenate([gap, rows], axis=0)
    part = jnp.where(core == 0, first, second).astype(BF)
    for k in range(GROUPS):
        wide[k] = part


def pack_kernel(order, count, tiles, x, cot, send, keep, state):
    state[...] = jnp.zeros_like(state)
    core = lax.axis_index("c")
    most = tiles.shape[1]
    on = []
    for tile in range(COLS // TILE):
        live = jnp.int32(0)
        for k in range(most):
            live = live | ((tiles[0, k] == tile) & (k < count[0])).astype(jnp.int32)
        on.append(live.astype(F32))
    row = lax.broadcasted_iota(jnp.int32, (TILE, CH), 0)
    marks = jnp.zeros((TILE, CH), F32)
    for tile, value in enumerate(on):
        marks = jnp.where(row == tile, value, marks)
    for target, slot in ((keep, core), (send, 1 - core)):
        target[:COLS] = x[order[slot]]
        for tile, value in enumerate(on):
            rows = cot[slot, tile * TILE : (tile + 1) * TILE].astype(F32) * value
            target[COLS + tile * TILE : COLS + (tile + 1) * TILE] = rows.astype(BF)
        target[2 * COLS :] = marks.astype(BF)


def arrange_kernel(keep, got, block, up, down, first):
    core = lax.axis_index("c")

    def place(one, two):
        block[:COLS] = one[:COLS]
        block[COLS : 2 * COLS] = two[:COLS]
        block[2 * COLS : 3 * COLS] = one[COLS : 2 * COLS]
        block[3 * COLS : 4 * COLS] = two[COLS : 2 * COLS]
        block[4 * COLS : 4 * COLS + TILE] = one[2 * COLS :]
        block[4 * COLS + TILE :] = two[2 * COLS :]
        for target in (up, down):
            target[:COLS] = one[:COLS]
            target[COLS : 2 * COLS] = two[:COLS]
        down[2 * COLS : 3 * COLS] = one[COLS : 2 * COLS]
        down[3 * COLS : 4 * COLS] = two[COLS : 2 * COLS]
        down[4 * COLS :] = one[2 * COLS :]
        first[...] = one[:COLS]

    @pl.when(core == 0)
    def _():
        place(keep, got)

    @pl.when(core == 1)
    def _():
        place(got, keep)


def position():
    chip = lax.axis_index("x") * lax.axis_size("z") + lax.axis_index("z")
    shifted = lax.axis_index("y") % 2 == 1
    return chip, shifted


def keep_factor(chips):
    chip, shifted = position()
    return jnp.where(shifted & (chip == chips - 1), 0.0, 1.0).astype(BF)


def prep_kernel(mine, other, bias, block, before, after, second, deriv, weights, x4, mask, x6):
    core = lax.axis_index("c")

    def assemble(even, odd):
        for k in range(GROUPS):
            base = 72 * k
            weights[base : base + 32] = even[k, 0:32]
            both = even[k, 32:40].astype(F32) + odd[k, 0:8].astype(F32)
            weights[base + 32 : base + 40] = both.astype(BF)
            weights[base + 40 : base + 72] = odd[k, 8:40]

    @pl.when(core == 0)
    def _():
        assemble(mine, other)

    @pl.when(core == 1)
    def _():
        assemble(other, mine)

    chip, shifted = position()
    aligned = jnp.logical_not(shifted)
    last = GROUPS - 1

    def rows(ref, j):
        return ref[j * COLS : (j + 1) * COLS]

    own0, own1 = rows(block, 0), rows(block, 1)
    next0, next1 = rows(after, 0), rows(after, 1)
    prev0, prev1 = rows(before, 0), rows(before, 1)
    zero = jnp.zeros((COLS, CH), BF)
    start = aligned & (chip == 0)
    end = aligned & (chip == last)
    cut0 = start | (shifted & (chip == 0))
    cut5 = end | (shifted & (chip == last - 1))
    x6[0] = jnp.where(cut0, zero, jnp.where(shifted, prev1, prev0))
    x6[1] = jnp.where(start, zero, jnp.where(shifted, own0, prev1))
    x6[2] = jnp.where(shifted, own1, own0)
    x6[3] = jnp.where(shifted, next0, own1)
    x6[4] = jnp.where(end, zero, jnp.where(shifted, next1, next0))
    x6[5] = jnp.where(cut5, zero, jnp.where(shifted, second[...], next1))

    own_marks = block[4 * COLS :].astype(F32)
    next_marks = after[4 * COLS :].astype(F32)
    for j in range(2):
        here = own_marks[j * TILE : (j + 1) * TILE]
        there = own_marks[TILE:] if j == 0 else next_marks
        marks = jnp.where(shifted, there, here)
        for tile in range(COLS // TILE):
            mask[j * COLS + tile * TILE : j * COLS + (tile + 1) * TILE] = jnp.broadcast_to(
                marks[tile : tile + 1], (TILE, CH)
            )

    for j in range(4):
        x4[j] = x6[1 + j]
    keep = keep_factor(GROUPS)
    lhs = [
        jnp.concatenate([x6[0], x6[1], x6[2] * keep, x6[3]], axis=0),
        jnp.concatenate([x6[1], x6[2], x6[3], x6[4]], axis=0),
        jnp.concatenate([x6[2], x6[3] * keep, x6[4], x6[5]], axis=0),
    ]
    shift = jnp.broadcast_to(bias[...], (COLS, CH))
    sums = []
    for b in range(3):
        total = None
        for a in range(3):
            tap = (3 * a + b) * CH
            term = jnp.dot(lhs[a], weights[tap : tap + CH], preferred_element_type=F32)
            total = term if total is None else total + term
        sums.append(total)
    for r in range(4):
        part = slice(r * COLS, (r + 1) * COLS)
        pre = from_left(sums[0][part]) + sums[1][part] + from_right(sums[2][part]) + shift
        sig = jax.nn.sigmoid(pre)
        value = sig * (1.0 + pre * (1.0 - sig))
        if r == 0:
            value = jnp.where(start, 0.0, value)
        if r == 3:
            value = jnp.where(end, 0.0, value)
        deriv[r] = value


def step_kernel(step, sections, mask, deriv, weights, *refs):
    arrived, state_in, outs = refs[:2], refs[2], refs[3:]
    state = outs[0]
    active = lax.axis_index("y") == sections - 1 - step

    @pl.when(jnp.logical_not(active))
    def _():
        state[...] = state_in[...]

    @pl.when(active)
    def _():
        keep = keep_factor(GROUPS)
        if step == 0:
            block, after = arrived
            sources = [(block, 2), (block, 3), (after, 2), (after, 3)]
        else:
            straight, side = arrived
            low, high = (side, straight) if step % 2 else (straight, side)
            sources = [(low, 0), (low, 1), (high, 0), (high, 1)]
        gpre = []
        for r, (ref, at) in enumerate(sources):
            upstream = ref[at * COLS : (at + 1) * COLS]
            gpre.append((upstream.astype(F32) * deriv[r]).astype(BF))
        state[0] = gpre[1]
        state[1] = gpre[2]
        lhs = [
            jnp.concatenate([gpre[2] * keep, gpre[3]], axis=0),
            jnp.concatenate([gpre[1], gpre[2]], axis=0),
            jnp.concatenate([gpre[0], gpre[1] * keep], axis=0),
        ]
        sums = []
        for b in range(3):
            total = None
            for a in range(3):
                tap = (3 * a + b) * CH
                term = lax.dot_general(
                    lhs[a],
                    weights[tap : tap + CH],
                    (((1,), (1,)), ((), ())),
                    preferred_element_type=F32,
                )
                total = term if total is None else total + term
            sums.append(total)
        for j in range(2):
            part = slice(j * COLS, (j + 1) * COLS)
            value = from_right(sums[0][part]) + sums[1][part] + from_left(sums[2][part])
            value = (value * mask[part]).astype(BF)
            state[2 + j] = value
            if step < sections - 1:
                outs[1][part] = value

    if step == sections - 1:
        for j in range(2):
            outs[1][j * COLS : (j + 1) * COLS] = state[j]


def grads_kernel(order, state, got, other, grads):
    core = lax.axis_index("c")
    _, shifted = position()
    grads[order[1 - core]] = got[...]
    mine = jnp.where(core == 0, other[...], state[2])
    grads[order[core]] = jnp.where(shifted, mine, state[2 + core])


def wgrad_kernel(x_own, x_other, state, g_other, parts, send, spill, total):
    core = lax.axis_index("c")
    _, shifted = position()
    send[...] = jnp.where(shifted == (core == 1), state[3], state[2])
    spill[...] = state[3]
    keep = keep_factor(GROUPS)
    rows = [state[0], state[1], g_other[:COLS], g_other[COLS:]]
    g = [value.astype(F32) for value in rows]
    moved = [
        jnp.concatenate([from_right(value) for value in g], axis=0).astype(BF),
        jnp.concatenate(rows, axis=0),
        jnp.concatenate([from_left(value) for value in g], axis=0).astype(BF),
    ]
    pairs = (x_own, x_other)
    lhs = [
        jnp.concatenate([v for x in pairs for v in (x[0], x[1] * keep)], axis=0),
        jnp.concatenate([v for x in pairs for v in (x[1], x[2])], axis=0),
        jnp.concatenate([v for x in pairs for v in (x[2] * keep, x[3])], axis=0),
    ]
    for a, x in enumerate(lhs):
        for b in range(3):
            tap = (3 * a + b) * CH
            total[tap : tap + CH] = lax.dot_general(
                x, moved[b], (((0,), (0,)), ((), ())), preferred_element_type=F32
            )
    bias = jnp.sum((g[0] + g[1]) + (g[2] + g[3]), axis=0, keepdims=True)
    high = bias.astype(BF).astype(F32)
    low = bias - high
    row = lax.broadcasted_iota(jnp.int32, (WIN, CH), 0)
    at = jnp.where(core == 0, PART, 0)
    for k in range(GROUPS):
        value = total[pl.ds(pl.multiple_of(72 * k + 32 * core, 8), WIN), :]
        value = jnp.where(row == at, high, value)
        parts[k] = jnp.where(row == at + 1, low, value).astype(BF)


def total_kernel(parts, wgrad, bgrad):
    core = lax.axis_index("c")
    me = (lax.axis_index("x") * lax.axis_size("z") + lax.axis_index("z")) * 2 + core
    value = parts[0].astype(F32)
    for k in range(1, GROUPS):
        value = value + parts[k].astype(F32)
    result = jnp.where(core == 0, value[:PART], value[WIN - PART :])
    half = CH // 2
    for j in range(2):
        wgrad[pl.ds(j, PART, stride=2), :] = result[:, j * half : (j + 1) * half]
    row = lax.broadcasted_iota(jnp.int32, (WIN, CH), 0)
    at = jnp.where(core == 0, PART, 0)
    here = (row == at) | (row == at + 1)
    bias = jnp.sum(jnp.where(here, value, 0.0), axis=0, keepdims=True)
    lane = lax.broadcasted_iota(jnp.int32, (1, CH), 1)
    spot = lax.broadcasted_iota(jnp.int32, (1, 4), 1)
    result = jnp.zeros((1, 4), F32)
    for j in range(4):
        one = jnp.sum(jnp.where(lane == 4 * me + j, bias, 0.0), axis=1, keepdims=True)
        result = jnp.where(spot == j, one, result)
    bgrad[...] = result


def chip_pairs(planes, by, down=0):
    return [
        (p * 64 + 2 * k + c, (p - down) * 64 + 2 * ((k + by) % GROUPS) + c)
        for p in planes
        for k in range(GROUPS)
        for c in range(2)
    ]


def return_pairs(sections):
    pairs = []
    for p in range(sections):
        for k in range(GROUPS):
            one, two = p * 64 + 2 * k, p * 64 + 2 * k + 1
            pairs.append((one, two))
            pairs.append((two, p * 64 + 2 * ((k + 1) % GROUPS)) if p % 2 else (two, one))
    return pairs


def body(saved_inputs, weights, biases, cotangent, tile_list, tile_count, order):
    sections = lax.axis_size("y")
    every = range(sections)
    shifts = range(1, sections, 2)
    image = (2, COLS, CH)
    inputs = saved_inputs.reshape(image)
    cot = cotangent.reshape(image)

    (wide,) = call(
        wide_kernel, [VMEM], [out((GROUPS, WIN, CH), BF)], (weights[0],), moved=1 << 20
    )
    swap = [(0, 1), (1, 0)]
    mine = lax.all_to_all(wide, ("x", "z"), 0, 0)

    send, keep, state = call(
        pack_kernel,
        [SMEM] * 3 + [VMEM] * 2,
        [out((2 * COLS + TILE, CH), BF)] * 2 + [out((4, COLS, CH), BF)],
        (order, tile_count, tile_list, inputs, cot),
        flops=1 << 28,
        moved=3 << 20,
    )
    got = lax.ppermute(send, "c", swap)
    block, up, down, first = call(
        arrange_kernel,
        [VMEM] * 2,
        [
            out((4 * COLS + 2 * TILE, CH), BF),
            out((2 * COLS, CH), BF),
            out((4 * COLS + TILE, CH), BF),
            out((COLS, CH), BF),
        ],
        (keep, got),
        flops=1 << 26,
        moved=1 << 20,
    )
    after = lax.ppermute(down, ALL, chip_pairs(every, -1))
    before = lax.ppermute(up, ALL, chip_pairs(every, 1))
    second = lax.ppermute(first, ALL, chip_pairs(shifts, -2))
    mine, after, before, second = lax.optimization_barrier((mine, after, before, second))
    other = lax.ppermute(mine, "c", swap)

    deriv, wfull, x4, mask = call(
        prep_kernel,
        [VMEM] * 7,
        [
            out((4, COLS, CH), F32),
            out((9 * CH, CH), BF),
            out((4, COLS, CH), BF),
            out((2 * COLS, CH), F32),
        ],
        (mine, other, biases, block, before, after, second),
        scratch=[pltpu.VMEM((6, COLS, CH), BF)],
        flops=1 << 30,
        moved=4 << 20,
    )

    arrived = [block, after]
    for step in range(sections):
        live = step < sections - 1
        state, back = call(
            lambda *refs, step=step: step_kernel(step, sections, *refs),
            [VMEM] * (4 + len(arrived)),
            [out((4, COLS, CH), BF), out((2 * COLS, CH), BF)],
            (mask, deriv, wfull, *arrived, state),
            aliases={3 + len(arrived): 0},
            flops=1 << 27,
            moved=2 << 20,
        )
        if live:
            plane = sections - 1 - step
            straight = lax.ppermute(back, ALL, chip_pairs([plane], 0, 1))
            side = lax.ppermute(back, ALL, chip_pairs([plane], 1 if plane % 2 else -1, 1))
            arrived = [straight, side]
        if step == 2:
            late, _ = lax.optimization_barrier((x4, back))
            x_other = lax.ppermute(late, "c", swap)

    g_other = lax.ppermute(back, "c", swap)
    both, send, spill = call(
        wgrad_kernel,
        [VMEM] * 4,
        [out((GROUPS, WIN, CH), BF)] + [out((COLS, CH), BF)] * 2,
        (x4, x_other, state, g_other),
        scratch=[pltpu.VMEM((9 * CH, CH), F32)],
        flops=1 << 28,
        moved=4 << 20,
    )
    got = lax.ppermute(send, ALL, return_pairs(sections))
    spilled = lax.ppermute(spill, ALL, chip_pairs(shifts, 1))
    (grads,) = call(
        grads_kernel,
        [SMEM] + [VMEM] * 3,
        [out(image, BF)],
        (order, state, got, spilled),
        moved=1 << 18,
    )
    parts = lax.all_to_all(both, ("x", "z"), 0, 0)
    wgrad, bgrad = call(
        total_kernel,
        [VMEM],
        [out((2 * PART, CH // 2), F32), out((1, 4), F32)],
        (parts,),
        moved=1 << 20,
    )
    return grads.reshape(1, 2, 1, COLS, CH), wgrad.reshape(1, PART, CH), bgrad


def solution(mesh):
    fine = Mesh(mesh.devices.reshape(8, 4, 8, 2), ALL)
    placed = (
        P("y", None, SEC, None, None),
        P("y", SEC, None),
        P("y", None),
        P(None, SEC, None, None),
        P(SEC, None),
        P(SEC),
        P(),
    )
    return jax.shard_map(
        body,
        mesh=fine,
        in_specs=placed,
        out_specs=(P("y", None, SEC, None, None), P("y", SEC, None), P("y", SEC)),
        check_vma=False,
    )
```
